128 devices in a mesh: src: 8 (over y, x_hi), reg: 16 (over z, x_lo, core).
Axes of the slice: x: 4 (x_hi: 2, x_lo: 2; x = x_hi * 2 + x_lo), y: 4, z: 4, core: 2. Of those that a mesh axis runs over, the one named last changes fastest.
Arguments:
- displacement: float32 [3, 5, 1024, 2048], P(None, None, 'src', 'reg'), may hold values from -0.06 to 0.06
- velocity: float32 [3, 5, 1024, 2048], P(None, None, 'src', 'reg'), may hold values from -6 to 6
- modulus: float32 [5, 1024, 2048], P(None, 'src', 'reg'), may hold values from 0.5 to 2
- density: float32 [5, 1024, 2048], P(None, 'src', 'reg'), may hold values from 0.8 to 1.25
- traces: float32 [128, 512, 9, 128], P(('src', 'reg')), may hold values from -18 to 18
- record_row: int32 [128, 512], P(('src', 'reg')), may hold values from 0 to 127, as said below
Outputs:
- final_displacement: float32 [3, 5, 1024, 2048], P(None, None, 'src', 'reg')
- final_velocity: float32 [3, 5, 1024, 2048], P(None, None, 'src', 'reg')
The draws below stay inside these ranges and needn't reach their ends.
Inputs may be any that keep to these rules, and one draw needn't show every extreme that they name: `record_row`: for every destination device d and step t, the entries of slots (d * 4 + t) + k, k < 1, taken over all segmenting buffers in order, form a permutation of 0 to 127.
All inputs are finite; a program needn't handle non-finite values.
Results may differ from the reference program's by a relative error of at most 0.000061.
Values sent between devices are 32-bit elements; how exact they have to be, the bound alone decides.
No kernel may reach another device: no remote copies, remote signals or barrier semaphores. Data moves between devices by JAX's collectives and lax.ppermute only.
A program may use at most 128 MiB of HBM per device.

```python
import math
import jax
import jax.numpy as jnp
import numpy as np
from jax import lax

EZ = 1
STEPS = 4
SOURCES = 128
XL = 128
RY = 128
RPS = 1
NX = 2048
NY = 1024
NZ = 5
N_SRC = 8
N_REG = 16


def draw_record_row(key, part):
    subkeys = jax.random.split(key, SOURCES * STEPS)
    orders = jax.vmap(lambda single: jax.random.permutation(single, RY))(subkeys)
    orders = orders.reshape(SOURCES, STEPS, SOURCES, RPS)
    orders = jnp.transpose(orders, (2, 0, 1, 3))
    return orders.reshape(SOURCES, SOURCES * STEPS * RPS).astype(jnp.int32)


def block_levels(rng, dims, shards, smallest, top_value):
    level = 1.0
    for axis_at, shards_of in shards:
        steps = jax.random.uniform(jax.random.fold_in(jax.random.fold_in(rng, 6), axis_at), (shards_of,), jnp.float32, smallest / len(shards), top_value / len(shards))
        level = level * jnp.repeat(jnp.exp(steps), dims[axis_at] // shards_of).reshape((-1,) + (1,) * (len(dims) - 1 - axis_at))
    return level


def bell_draw(own_key, dims, scale, limit, shards=(), held_as=jnp.bfloat16):
    values = scale * jax.random.normal(own_key, dims, jnp.float32)
    if shards:
        values = values * block_levels(own_key, dims, shards, -0.22, 0.18)
    return jnp.clip(values, -limit, limit).astype(held_as)


def setup_inputs(seed: int = 0) -> dict:
    key_of = jax.random.split(jax.random.key(seed), 7)
    return {
        "displacement": bell_draw(key_of[0], (3, NZ, NY, NX), 0.01, 0.06, ((2, 8), (3, 16)), jnp.float32),
        "velocity": bell_draw(key_of[1], (3, NZ, NY, NX), 1.0, 6.0, ((2, 8), (3, 16)), jnp.float32),
        "modulus": jnp.clip(jnp.exp(math.log(2.0) - 1.3862944 * jax.random.uniform(key_of[2], (NZ, NY, NX), jnp.float32) ** block_levels(key_of[2], (NZ, NY, NX), ((1, 8), (2, 16)), -0.2, 0.2)), 0.5, 2.0),
        "density": jnp.clip(0.8 + 0.45 * jax.random.uniform(key_of[3], (NZ, NY, NX), jnp.float32) ** block_levels(key_of[3], (NZ, NY, NX), ((1, 8), (2, 16)), -0.2, 0.2), 0.8, 1.25),
        "traces": bell_draw(key_of[4], (SOURCES, SOURCES * STEPS * RPS, 9, XL), 3.0, 18.0, ((0, 128),), jnp.float32),
        "record_row": draw_record_row(jax.random.fold_in(key_of[6], 71), 0),
    }


time_step = 0.02

def gll_tables():
    inner_node = math.sqrt(3.0 / 7.0)
    gll_nodes = np.array([-1.0, -inner_node, 0.0, inner_node, 1.0])
    weights = np.array([0.1, 49.0 / 90.0, 32.0 / 45.0, 49.0 / 90.0, 0.1])
    legendre = (35.0 * gll_nodes ** 4 - 30.0 * gll_nodes ** 2 + 3.0) / 8.0
    derivative = np.zeros((5, 5))
    for target in range(5):
        for source in range(5):
            if target != source:
                derivative[target, source] = legendre[target] / (legendre[source] * (gll_nodes[target] - gll_nodes[source]))
    derivative[0, 0] = -5.0
    derivative[4, 4] = 5.0
    return (derivative, weights)

def periodic_weights(length):
    derivative, weights = gll_tables()
    pattern = np.array([2.0 * weights[0], weights[1], weights[2], weights[3]])
    return np.tile(pattern, length // 4)

def bounded_weights(elements):
    derivative, weights = gll_tables()
    result = np.zeros(4 * elements + 1)
    for element in range(elements):
        result[4 * element:4 * element + 5] += weights
    return result

def split_elements(values, line_axis):
    length = values.shape[line_axis]
    elements = (length - 1) // 4
    old_shape = values.shape
    leading = lax.slice_in_dim(values, 0, length - 1, axis=line_axis)
    leading = leading.reshape(old_shape[:line_axis] + (elements, 4) + old_shape[line_axis + 1:])
    closing = lax.slice_in_dim(values, 4, length, stride=4, axis=line_axis)
    closing = jnp.expand_dims(closing, line_axis + 1)
    return jnp.concatenate([leading, closing], axis=line_axis + 1)

def apply_matrix(blocks, matrix, line_axis):
    position = line_axis + 1
    fac_shape = [1] * blocks.ndim
    fac_shape[position] = 5
    result = None
    for column in range(5):
        factor = jnp.asarray(matrix[:, column], jnp.float32).reshape(fac_shape)
        product_term = factor * lax.index_in_dim(blocks, column, position, keepdims=True)
        result = product_term if result is None else result + product_term
    return result

def assemble(blocks, line_axis):
    position = line_axis + 1
    old_shape = blocks.shape
    elements = old_shape[line_axis]
    leading = lax.slice_in_dim(blocks, 0, 4, axis=position)
    leading = leading.reshape(old_shape[:line_axis] + (4 * elements,) + old_shape[position + 1:])
    closing = lax.index_in_dim(blocks, 4, position, keepdims=False)
    zero_one = jnp.zeros_like(lax.slice_in_dim(closing, 0, 1, axis=line_axis))
    assembled = jnp.concatenate([leading, zero_one], axis=line_axis)
    shifted = jnp.concatenate([zero_one, closing], axis=line_axis)
    spread = jnp.expand_dims(lax.slice_in_dim(shifted, 0, elements, axis=line_axis), position)
    pad_shape = list(spread.shape)
    pad_shape[position] = 3
    padding = jnp.zeros(pad_shape, spread.dtype)
    spread = jnp.concatenate([spread, padding], axis=position).reshape(leading.shape)
    spread = jnp.concatenate([spread, lax.slice_in_dim(shifted, elements, elements + 1, axis=line_axis)], axis=line_axis)
    return assembled + spread

def line_stiffness(values, coefficient, line_axis):
    derivative, weights = gll_tables()
    blocks = split_elements(values, line_axis)
    coefficient_blocks = split_elements(coefficient, line_axis)
    slopes = apply_matrix(blocks, derivative, line_axis)
    quad_shape = [1] * blocks.ndim
    quad_shape[line_axis + 1] = 5
    quadrature = jnp.asarray(weights, jnp.float32).reshape(quad_shape)
    fluxes = slopes * coefficient_blocks * quadrature
    tested = apply_matrix(fluxes, derivative.T, line_axis)
    return assemble(tested, line_axis)

def wrap_line(values, line_axis):
    length = values.shape[line_axis]
    return jnp.concatenate([lax.slice_in_dim(values, length - 4, length, axis=line_axis), values, lax.slice_in_dim(values, 0, 1, axis=line_axis)], axis=line_axis)

def periodic_term(values, coefficient, line_axis):
    length = values.shape[line_axis]
    extended = line_stiffness(wrap_line(values, line_axis), wrap_line(coefficient, line_axis), line_axis)
    return lax.slice_in_dim(extended, 4, 4 + length, axis=line_axis)

def reference(displacement, velocity, modulus, density, traces, record_row):
    east_weight = jnp.asarray(periodic_weights(NX), jnp.float32)[None, None, :]
    north_weight = jnp.asarray(periodic_weights(NY), jnp.float32)[None, :, None]
    depth_weight = jnp.asarray(bounded_weights(EZ), jnp.float32)[:, None, None]
    stiff_east = (0.5 * modulus * north_weight * depth_weight)[None]
    stiff_north = (0.5 * modulus * east_weight * depth_weight)[None]
    stiff_depth = (0.5 * modulus * east_weight * north_weight)[None]
    inverse = 1.0 / (0.125 * density * east_weight * north_weight * depth_weight)
    bottom_area = 0.25 * east_weight[0] * north_weight[0]
    impedance = jnp.sqrt(density[0] * modulus[0])
    spring = 0.5 * modulus[0]
    records = traces.reshape(SOURCES, SOURCES, STEPS, RPS, 9, XL)
    row_ids = record_row.reshape(SOURCES, SOURCES, STEPS, RPS)
    target_ids = jnp.broadcast_to(jnp.arange(SOURCES, dtype=jnp.int32)[None, :, None, None], row_ids.shape)
    step_ids = jnp.broadcast_to(jnp.arange(STEPS, dtype=jnp.int32)[None, None, :, None], row_ids.shape)
    gathered = jnp.zeros((SOURCES, STEPS, RY, 9, XL), jnp.float32).at[target_ids, step_ids, row_ids].set(records)
    gathered = gathered.reshape(N_SRC, N_REG, STEPS, RY, 9, XL)
    injected = jnp.transpose(gathered, (2, 4, 0, 3, 1, 5)).reshape(STEPS, 9, NY, NX)
    for step_index in range(STEPS):
        previous_velocity = velocity
        displacement = displacement + time_step * velocity
        forces = -(periodic_term(displacement, stiff_east, 3) + periodic_term(displacement, stiff_north, 2) + line_stiffness(displacement, stiff_depth, 1))
        incoming = injected[step_index]
        bottom = bottom_area * (incoming[:3] + impedance * (incoming[3:6] - previous_velocity[:, 0]) + spring * (incoming[6:] - displacement[:, 0]))
        forces = forces.at[:, 0].add(bottom)
        velocity = velocity + time_step * (forces * inverse)
    return (displacement, velocity)
```

```python
import math

import jax
import jax.numpy as jnp
import numpy as np
from jax import lax
from jax.experimental import pallas as pl
from jax.experimental.pallas import tpu as pltpu
from jax.sharding import PartitionSpec as P


F32 = jnp.float32
BF16 = jnp.bfloat16
STEPS = 4
DT = 0.02
N = 128
H = 16
E = 40
FORCE_ROWS = ((12, 0), (8, 12), (4, 20))
VMEM_LIMIT = 28 * 1024 * 1024


def gll():
    inner = math.sqrt(3.0 / 7.0)
    x = np.array([-1.0, -inner, 0.0, inner, 1.0])
    w = np.array([0.1, 49.0 / 90.0, 32.0 / 45.0, 49.0 / 90.0, 0.1])
    leg = (35.0 * x**4 - 30.0 * x**2 + 3.0) / 8.0
    d = np.zeros((5, 5))
    for i in range(5):
        for j in range(5):
            if i != j:
                d[i, j] = leg[i] / (leg[j] * (x[i] - x[j]))
    d[0, 0] = -5.0
    d[4, 4] = 5.0
    return d, w


DER, W = gll()
BACK = (DER * W[:, None]).T
PERIODIC = [2 * W[0], W[1], W[2], W[3]]


def apply5(m, v):
    s0, s1, m0, m1 = v[0] + v[4], v[1] + v[3], v[0] - v[4], v[1] - v[3]
    f = lambda a: float(np.float32(a))
    out = [None] * 5
    for i in (0, 1):
        p = f((m[i, 0] - m[i, 4]) / 2) * m0 + f((m[i, 1] - m[i, 3]) / 2) * m1
        q = f((m[i, 0] + m[i, 4]) / 2) * s0 + f((m[i, 1] + m[i, 3]) / 2) * s1 + f(m[i, 2]) * v[2]
        out[i], out[4 - i] = p + q, p - q
    out[2] = f(m[2, 0]) * m0 + f(m[2, 1]) * m1
    return out


def column_of(x, comp):
    if 0 <= x < N:
        return x
    return N + 32 * comp + (x - N if x >= N else x + 32)


def east_tables():
    grad = np.zeros((3, 256, 256))
    sel = np.zeros((256, 256))
    weight = np.zeros((1, 256))
    for k in range(E):
        for i in range(5):
            q = i * E + k
            xi = 4 * (k - 4) + i
            weight[0, q] = 0.5 * W[i]
            if xi < N + H:
                sel[column_of(xi, 0), q] = 1.0
            for comp in range(3):
                for j in range(5):
                    xj = 4 * (k - 4) + j
                    if xj < N + H:
                        grad[comp, column_of(xj, comp), q] = DER[i, j]

    def two(a):
        hi = a.astype(np.float32).astype(jnp.bfloat16)
        lo = (a - hi.astype(np.float64)).astype(np.float32).astype(jnp.bfloat16)
        return np.stack([hi, lo], axis=1)

    back = np.ascontiguousarray(np.swapaxes(grad, 1, 2))
    return two(grad), two(back), sel.astype(jnp.bfloat16), weight.astype(np.float32)


def shifted(block, axis, distance):
    n = lax.axis_size(axis)
    return lax.ppermute(block, axis, [((i - distance) % n, i) for i in range(n)])


def in_hbm(*arrays):
    return [pltpu.with_memory_space_constraint(x, pltpu.HBM) for x in arrays]


def dot(a, b):
    return jnp.dot(a, b, preferred_element_type=F32)


def split2(x):
    hi = x.astype(BF16)
    return hi, (x - hi.astype(F32)).astype(BF16)


def lane_ids(shape):
    return lax.broadcasted_iota(jnp.int32, shape, len(shape) - 1)


def east_weight(shape):
    r = lane_ids(shape) % 4
    f = lambda a: float(np.float32(a))
    return jnp.where(r == 0, f(PERIODIC[0]), jnp.where(r == 2, f(PERIODIC[2]), f(PERIODIC[1])))


def lane_move(x, shift, start, width=16):
    shift %= 128
    y = pltpu.roll(x, shift, x.ndim - 1) if shift else x
    lane = lane_ids(x.shape)
    return jnp.where((lane >= start) & (lane < start + width), y, 0.0)


def pack_kernel(tr_ref, id_ref, out_ref, buf, in_sem, out_sem):
    copy = pltpu.make_async_copy
    part = N // 4
    loads = []
    for q in range(4):
        at = pl.ds(q * part, part)
        loads.append(
            [
                copy((tr_ref.at[k, at] if k < 9 else id_ref.at[at]), buf.at[at, k], in_sem.at[q, k])
                for k in range(10)
            ]
        )
        for c in loads[q]:
            c.start()
    stores = []
    for q in range(4):
        for c in loads[q]:
            c.wait()
        at = pl.ds(q * part, part)
        stores.append(copy(buf.at[at], out_ref.at[at], out_sem.at[q]))
        stores[q].start()
    for c in stores:
        c.wait()


def pack(records, rows):
    return pl.pallas_call(
        pack_kernel,
        in_specs=[pl.BlockSpec(memory_space=pltpu.HBM)] * 2,
        out_specs=pl.BlockSpec(memory_space=pltpu.HBM),
        out_shape=pltpu.HBM((128, 10, STEPS, 128), F32),
        scratch_shapes=[
            pltpu.VMEM((N, 10, STEPS, N), F32),
            pltpu.SemaphoreType.DMA((4, 10)),
            pltpu.SemaphoreType.DMA((4,)),
        ],
        compiler_params=pltpu.CompilerParams(vmem_limit_bytes=8 * 1024 * 1024),
        name="pack",
    )(*in_hbm(records, rows))


def strips_kernel(
    d_ref, v_ref, m_ref, r_ref, west_ref, east_ref, north_ref, south_ref, ln_ref, ls_ref,
    buf, west_buf, east_buf, in_sem, row_sem, out_sem,
):
    copy = pltpu.make_async_copy
    loads = []
    for z in range(5):
        loads.append(
            [
                copy(d_ref.at[:, z], buf.at[z, 0:3], in_sem.at[z, 0]),
                copy(v_ref.at[:, z], buf.at[z, 3:6], in_sem.at[z, 1]),
                copy(m_ref.at[z], buf.at[z, 6], in_sem.at[z, 2]),
                copy(r_ref.at[z], buf.at[z, 7], in_sem.at[z, 3]),
            ]
        )
        for c in loads[z]:
            c.start()
    lane = lane_ids((N, N))
    stores = []
    for z in range(5):
        for c in loads[z]:
            c.wait()
        for i, (at, top, low) in enumerate(
            ((slice(0, 6), north_ref, south_ref), (slice(6, 8), ln_ref, ls_ref))
        ):
            stores.append(copy(buf.at[z, at, N - H : N], top.at[:, z], row_sem.at[z, 2 * i]))
            stores.append(copy(buf.at[z, at, 0:H], low.at[:, z], row_sem.at[z, 2 * i + 1]))
        for c in stores[-4:]:
            c.start()
        west = buf[z, 0]
        east = pltpu.roll(west, N - 112, 1)
        for a in range(1, 8):
            x = buf[z, a]
            west = jnp.where(lane < 16 * a, west, pltpu.roll(x, 16 * a, 1))
            east = jnp.where(
                lane < 16 * a, east, pltpu.roll(x, (16 * a - 112) % N, 1) if a != 7 else x
            )
        west_buf[z] = west
        east_buf[z] = east
        stores.append(copy(west_buf.at[z], west_ref.at[z], out_sem.at[z, 0]))
        stores.append(copy(east_buf.at[z], east_ref.at[z], out_sem.at[z, 1]))
        for c in stores[-2:]:
            c.start()
    for c in stores:
        c.wait()


def strips(d, v, m, r):
    hbm = pl.BlockSpec(memory_space=pltpu.HBM)
    dma = pltpu.SemaphoreType.DMA
    return pl.pallas_call(
        strips_kernel,
        in_specs=[hbm] * 4,
        out_specs=[hbm] * 6,
        out_shape=[pltpu.HBM((5, N, N), F32)] * 2
        + [pltpu.HBM((6, 5, H, N), F32)] * 2
        + [pltpu.HBM((2, 5, H, N), F32)] * 2,
        scratch_shapes=[
            pltpu.VMEM((5, 8, N, N), F32),
            pltpu.VMEM((5, N, N), F32),
            pltpu.VMEM((5, N, N), F32),
            dma((5, 4)),
            dma((5, 4)),
            dma((5, 2)),
        ],
        compiler_params=pltpu.CompilerParams(vmem_limit_bytes=16 * 1024 * 1024),
        name="strips",
    )(*in_hbm(d, v, m, r))


def place_kernel(
    arr_ref, mod_ref, rho_ref, b_ref, west_ref, east_ref, inj_ref, last_ref, m_ref, r_ref, vid_ref, ids_ref, sem
):
    own = [
        pltpu.make_async_copy(mod_ref.at[0:1], m_ref, sem.at[0]),
        pltpu.make_async_copy(rho_ref.at[0:1], r_ref, sem.at[1]),
    ]
    for c in own:
        c.start()
    vid_ref[...] = arr_ref[:, 36, :].astype(jnp.int32)
    to_scalar = pltpu.make_async_copy(vid_ref, ids_ref, sem.at[2])
    to_scalar.start()
    to_scalar.wait()
    for c in own:
        c.wait()

    def body(s, carry):
        for t in range(STEPS):
            r = ids_ref[s, t]
            at = pl.multiple_of((t * N + r) * 8, 8)
            inj_ref[pl.ds(at, 8), :] = arr_ref[s, pl.ds(t, 8, stride=4), :]
            last_ref[pl.ds(t * N + r, 1), :] = arr_ref[s, 32 + t : 33 + t, :]
        return carry

    lax.fori_loop(0, 128, body, 0, unroll=8)
    ew = east_weight((8, N))
    row = lax.broadcasted_iota(jnp.int32, (8, N), 0) % 4
    f = lambda a: float(np.float32(a))
    nw = jnp.where(row == 0, f(PERIODIC[0]), jnp.where(row == 2, f(PERIODIC[2]), f(PERIODIC[1])))
    area = 0.25 * ew * nw

    def combine(k, carry):
        y = pl.multiple_of(k * 8, 8)
        mod = m_ref[0, pl.ds(y, 8), :]
        imp = jnp.sqrt(r_ref[0, pl.ds(y, 8), :] * mod)
        spring = 0.5 * mod
        for t in range(STEPS):
            west = east = None
            for c in range(3):
                base = (t * N + y) * 8
                inc = inj_ref[pl.ds(base + c, 8, stride=8), :]
                vel = inj_ref[pl.ds(base + 3 + c, 8, stride=8), :]
                if c < 2:
                    dis = inj_ref[pl.ds(base + 6 + c, 8, stride=8), :]
                else:
                    dis = last_ref[pl.ds(t * N + y, 8), :]
                b = area * (inc + imp * vel + spring * dis)
                b_ref[t, c, pl.ds(y, 8), :] = b
                if t < 3:
                    w = lane_move(b, 32 * c, 32 * c)
                    e = lane_move(b, 32 * c + 16 - 112, 32 * c + 16)
                    west = w if c == 0 else west + w
                    east = e if c == 0 else east + e
            if t < 3:
                west_ref[t, pl.ds(y, 8), :] = west
                east_ref[t, pl.ds(y, 8), :] = east
        return carry

    lax.fori_loop(0, 16, combine, 0)


def place(arrived, mod, rho):
    whole = pl.BlockSpec(memory_space=pltpu.VMEM)
    hbm = pl.BlockSpec(memory_space=pltpu.HBM)
    return pl.pallas_call(
        place_kernel,
        in_specs=[whole, hbm, hbm],
        out_specs=[whole] * 3,
        out_shape=[
            jax.ShapeDtypeStruct((STEPS, 3, N, N), F32),
            jax.ShapeDtypeStruct((3, N, N), F32),
            jax.ShapeDtypeStruct((3, N, N), F32),
        ],
        scratch_shapes=[
            pltpu.VMEM((STEPS * N * 8, N), F32),
            pltpu.VMEM((STEPS * N, N), F32),
            pltpu.VMEM((1, N, N), F32),
            pltpu.VMEM((1, N, N), F32),
            pltpu.VMEM((N, N), jnp.int32),
            pltpu.SMEM((N, N), jnp.int32),
            pltpu.SemaphoreType.DMA((3,)),
        ],
        compiler_params=pltpu.CompilerParams(vmem_limit_bytes=VMEM_LIMIT),
        name="place",
    )(arrived, *in_hbm(mod, rho))


def rows_kernel(b_ref, e_ref, w_ref, strip_ref, north_ref, south_ref):
    for t in range(3):
        s = e_ref[t] + w_ref[t]
        strip_ref[t] = s
        n, at = FORCE_ROWS[t]
        for ch in range(4):
            x = b_ref.at[t, ch] if ch < 3 else strip_ref.at[t]
            north_ref[ch, at : at + n] = x[N - n :, :]
            south_ref[ch, at : at + n] = x[:n, :]


def force_rows(b, from_east, from_west):
    whole = pl.BlockSpec(memory_space=pltpu.VMEM)
    return pl.pallas_call(
        rows_kernel,
        in_specs=[whole] * 3,
        out_specs=[whole] * 3,
        out_shape=[
            jax.ShapeDtypeStruct((3, N, N), F32),
            jax.ShapeDtypeStruct((4, 24, N), F32),
            jax.ShapeDtypeStruct((4, 24, N), F32),
        ],
        compiler_params=pltpu.CompilerParams(vmem_limit_bytes=VMEM_LIMIT),
        name="force_rows",
    )(b, from_east, from_west)


def line_forces(d, k, kn, mn_ref, ce_ref, grad_ref, back_ref, channels, emit):
    rows = 5 * 4 * E

    def north(ch):
        m = ch // 3
        for z in range(5):
            v = [d[ch][z, j] for j in range(4)]
            v.append(pltpu.roll(v[0], E - 1, 0))
            g = apply5(DER, v)
            r = apply5(BACK * W[z], [g[i] * mn_ref[m, z, i] for i in range(5)])
            r[0] = r[0] + pltpu.roll(r[4], 1, 0)
            for j in range(4):
                kn[ch][z, j] = r[j]

    def depth(ch):
        m = ch // 3
        for j in range(4):
            x = [d[ch][z, j] for z in range(5)]
            g = apply5(DER, x)
            r = apply5(BACK * PERIODIC[j], [g[z] * mn_ref[m, z, j] for z in range(5)])
            for z in range(5):
                emit(ch, j, z, x[z], (k[ch][z, j] + kn[ch][z, j]) + r[z])

    sh, sl = split2(d[3][...].reshape(rows, N))
    strip = None
    for c in range(3):
        mh, ml = split2(d[c][...].reshape(rows, N))
        hi = jnp.concatenate([mh, sh], axis=1)
        lo = jnp.concatenate([ml, sl], axis=1)
        g = dot(hi, grad_ref[c, 0]) + dot(lo, grad_ref[c, 0]) + dot(hi, grad_ref[c, 1])
        fh, fl = split2(g * ce_ref[...])
        f = dot(fh, back_ref[c, 0]) + dot(fl, back_ref[c, 0]) + dot(fh, back_ref[c, 1])
        k[c][...] = f[:, :N].reshape(5, 4, E, N)
        if channels == 4:
            strip = f[:, N:] if strip is None else strip + f[:, N:]
        north(c)
        if c:
            depth(c - 1)
    if channels == 4:
        north(3)
        k[3][...] = strip.reshape(5, 4, E, N)
    depth(2)
    if channels == 4:
        depth(3)


def prepare_kernel(
    d_in, v_in, m_in, r_in, re_ref, rw_ref, n_ref, s_ref, cn_ref, cs_ref, sel_ref, qw_ref, grad_ref, back_ref,
    d0, d1, d2, d3, v0, v1, v2, v3, mn_ref, di_ref, ce_ref, ai_ref, as_ref,
    k0, k1, k2, k3, n0, n1, n2, n3, mod_ref,
):
    d_ref, v_ref = (d0, d1, d2, d3), (v0, v1, v2, v3)
    f = lambda a: float(np.float32(a))
    shape = (E, N)
    ew = east_weight(shape)
    lane = lane_ids(shape)

    def ext(own, at, j, north=n_ref, south=s_ref):
        halo = (*at, pl.ds(j, 4, stride=4), slice(None))
        return jnp.concatenate([own(j), north[halo], south[halo]], axis=0)

    for z in range(5):
        for j in range(4):
            own = lambda ref, *at: lambda j: ref[(*at, pl.ds(j, 32, stride=4), slice(None))]
            xe = ext(own(re_ref, z), (2, z), j, cn_ref, cs_ref)
            xw = ext(own(rw_ref, z), (3, z), j, cn_ref, cs_ref)

            def strip(src, step):
                out = None
                for c in range(3):
                    p = lane_move(xe, 32 * c - src - step * c, 32 * c)
                    p = p + lane_move(xw, 32 * c + 16 - src - step * c, 32 * c + 16)
                    out = p if out is None else out + p
                return out

            v_all, d_all = [], []
            for c in range(3):
                d_all.append(ext(own(d_in, c, z), (c, z), j))
                v_all.append(ext(own(v_in, c, z), (3 + c, z), j))
            d_all.append(strip(0, 16))
            v_all.append(strip(48, 16))
            for ch in range(4):
                v_ref[ch][z, j] = v_all[ch]
                d_ref[ch][z, j] = d_all[ch] + DT * v_all[ch]
            mods = [ext(own(m_in, z), (0, z), j, cn_ref, cs_ref), strip(96, 0)]
            rhos = [ext(own(r_in, z), (1, z), j, cn_ref, cs_ref), jnp.where(lane < 96, strip(112, 0), 1.0)]
            for m in range(2):
                mod_ref[m, z, j] = mods[m]
                mn = 0.5 * mods[m] * ew
                mn_ref[m, z, j] = mn
                if j == 0:
                    mn_ref[m, z, 4] = pltpu.roll(mn, E - 1, 0)
                nd = f(PERIODIC[j]) * f(W[z])
                di_ref[m, z, j] = DT / (0.125 * rhos[m] * ew * nd)
                if z == 0:
                    area = 0.25 * ew * f(PERIODIC[j])
                    ai_ref[m, j] = area * jnp.sqrt(rhos[m] * mods[m])
                    as_ref[m, j] = area * (0.5 * mods[m])
    for z in range(5):
        x = jnp.concatenate(
            [mod_ref[0, z].reshape(4 * E, N), mod_ref[1, z].reshape(4 * E, N)], axis=1
        )
        hi = x.astype(BF16)
        x = x - hi.astype(F32)
        mid, lo = split2(x)
        c = dot(hi, sel_ref[...]) + dot(mid, sel_ref[...]) + dot(lo, sel_ref[...])
        c = c * (qw_ref[...] * f(W[z]))
        for j in range(4):
            at = (z * 4 + j) * E
            ce_ref[at : at + E, :] = c[j * E : j * E + E] * f(PERIODIC[j])

    def emit(ch, j, z, d, k):
        m = ch // 3
        v = v_ref[ch][z, j]
        if z == 0:
            k = k + ai_ref[m, j] * v + as_ref[m, j] * d
        v_ref[ch][z, j] = v - di_ref[m, z, j] * k

    line_forces(
        d_ref, (k0, k1, k2, k3), (n0, n1, n2, n3), mn_ref, ce_ref, grad_ref, back_ref, 4, emit
    )


def prepare(d, v, m, r, re, rw, rn, rs, cn, cs, tables):
    grad, back, sel, qw = tables
    whole = pl.BlockSpec(memory_space=pltpu.VMEM)
    state = jax.ShapeDtypeStruct((5, 4, E, N), F32)
    return pl.pallas_call(
        prepare_kernel,
        in_specs=[whole] * 14,
        out_specs=[whole] * 13,
        out_shape=[
            *[state] * 8,
            jax.ShapeDtypeStruct((2, 5, 5, E, N), F32),
            jax.ShapeDtypeStruct((2, 5, 4, E, N), F32),
            jax.ShapeDtypeStruct((5 * 4 * E, 256), F32),
            jax.ShapeDtypeStruct((2, 4, E, N), F32),
            jax.ShapeDtypeStruct((2, 4, E, N), F32),
        ],
        scratch_shapes=[pltpu.VMEM((5, 4, E, N), F32)] * 8 + [pltpu.VMEM((2, 5, 4, E, N), F32)],
        compiler_params=pltpu.CompilerParams(vmem_limit_bytes=VMEM_LIMIT),
        name="prepare",
    )(d, v, m, r, re, rw, rn, rs, cn, cs, sel, qw, grad, back)


def steps_kernel(
    i0, i1, i2, i3, u0, u1, u2, u3, mn_ref, di_ref, ce_ref, ai_ref, as_ref,
    b_ref, bs_ref, bn_ref, bo_ref, grad_ref, back_ref,
    dout_ref, vout_ref,
    d0, d1, d2, d3, v0, v1, v2, v3, k0, k1, k2, k3, n0, n1, n2, n3, f_ref,
):
    d_in, v_in = (i0, i1, i2, i3), (u0, u1, u2, u3)
    d_ref, v_ref = (d0, d1, d2, d3), (v0, v1, v2, v3)
    k_ref, kn_ref = (k0, k1, k2, k3), (n0, n1, n2, n3)
    for t in range(3):
        n, at = FORCE_ROWS[t]
        gap = jnp.zeros((8 - n // 2, N), F32)
        for ch in range(4):
            for j in range(4):
                own = pl.ds(j, 32, stride=4)
                x = b_ref[t, ch, own, :] if ch < 3 else bs_ref[t, own, :]
                halo = pl.ds(at + j, n // 4, stride=4)
                f_ref[t, ch, j] = jnp.concatenate(
                    [x, bn_ref[ch, halo, :], gap, bo_ref[ch, halo, :]], axis=0
                )
    for ch in range(3):
        for j in range(4):
            x = b_ref[3, ch, pl.ds(j, 32, stride=4), :]
            f_ref[3, ch, j] = jnp.concatenate([x, jnp.zeros((8, N), F32)], axis=0)

    for ch in range(4):
        for j in range(4):
            for z in range(5):
                v = v_in[ch][z, j]
                if z == 0:
                    v = v + di_ref[ch // 3, z, j] * f_ref[0, ch, j]
                v_ref[ch][z, j] = v
                d_ref[ch][z, j] = d_in[ch][z, j] + DT * v

    def velocity(t, ch, j, z, d, k):
        m = ch // 3
        v = v_ref[ch][z, j]
        if z == 0:
            k = k + ai_ref[m, j] * v + as_ref[m, j] * d - f_ref[t, ch, j]
        return v - di_ref[m, z, j] * k

    def step(t, carry):
        def emit(ch, j, z, d, k):
            v = velocity(t, ch, j, z, d, k)
            v_ref[ch][z, j] = v
            d_ref[ch][z, j] = d + DT * v

        line_forces(d_ref, k_ref, kn_ref, mn_ref, ce_ref, grad_ref, back_ref, 4, emit)
        return carry

    lax.fori_loop(1, 3, step, 0)

    def final(ch, j, z, d, k):
        dout_ref[ch, z, pl.ds(j, 32, stride=4), :] = d[:32]
        vout_ref[ch, z, pl.ds(j, 32, stride=4), :] = velocity(3, ch, j, z, d, k)[:32]

    line_forces(d_ref, k_ref, kn_ref, mn_ref, ce_ref, grad_ref, back_ref, 3, final)


def steps(prepared, b, bs, bn, bo, tables):
    grad, back = tables[:2]
    whole = pl.BlockSpec(memory_space=pltpu.VMEM)
    return pl.pallas_call(
        steps_kernel,
        in_specs=[whole] * 19,
        out_specs=[whole] * 2,
        out_shape=[jax.ShapeDtypeStruct((3, 5, N, N), F32)] * 2,
        scratch_shapes=[pltpu.VMEM((5, 4, E, N), F32)] * 16 + [pltpu.VMEM((4, 4, 4, E, N), F32)],
        compiler_params=pltpu.CompilerParams(vmem_limit_bytes=VMEM_LIMIT),
        name="steps",
    )(*prepared, b, bs, bn, bo, grad, back)


def local(displacement, velocity, modulus, density, traces, record_row):
    tables = tuple(jnp.asarray(t) for t in east_tables())
    west, east, north, south, late_north, late_south = strips(
        displacement, velocity, modulus, density
    )
    from_east = shifted(west, "reg", -1)
    from_west = shifted(east, "reg", 1)
    from_north = shifted(south, "src", -1)
    from_south = shifted(north, "src", 1)
    rows = record_row.reshape(N, 1, STEPS).astype(F32)
    rows = jnp.pad(rows, ((0, 0), (0, STEPS - 1), (0, N - STEPS)))
    records = jnp.transpose(traces[0], (1, 0, 2)).reshape(9, N, STEPS, N)
    sent = pack(records, rows)
    arrived = lax.all_to_all(sent, ("src", "reg"), split_axis=0, concat_axis=0, tiled=True)
    arrived = arrived.reshape(N, 40, N)
    corner = jnp.stack([from_east, from_west])
    late_south = jnp.concatenate([late_south, corner[:, :, :H]], axis=0)
    late_north = jnp.concatenate([late_north, corner[:, :, N - H :]], axis=0)
    corner_north = shifted(late_south, "src", -1)
    corner_south = shifted(late_north, "src", 1)
    b, b_west, b_east = place(arrived, modulus, density)
    b_from_east = shifted(b_west, "reg", -1)
    b_from_west = shifted(b_east, "reg", 1)
    from_north, from_south, corner_north, corner_south, _ = lax.optimization_barrier(
        (from_north, from_south, corner_north, corner_south, b)
    )
    prepared = prepare(
        displacement, velocity, modulus, density, from_east, from_west,
        from_north, from_south, corner_north, corner_south, tables,
    )
    b_strip, b_north, b_south = force_rows(b, b_from_east, b_from_west)
    b_from_south = shifted(b_north, "src", 1)
    b_from_north = shifted(b_south, "src", -1)
    return steps(prepared, b, b_strip, b_from_north, b_from_south, tables)


def solution(mesh):
    state = P(None, None, "src", "reg")
    field = P(None, "src", "reg")
    in_specs = (state, state, field, field, P(("src", "reg"), None, None, None), P(("src", "reg"), None))
    return jax.shard_map(local, mesh=mesh, in_specs=in_specs, out_specs=(state, state), check_vma=False)
```

```python
import math

import jax
import jax.numpy as jnp
import numpy as np
from jax import lax
from jax.experimental import pallas as pl
from jax.experimental.pallas import tpu as pltpu
from jax.sharding import PartitionSpec as P


F32 = jnp.float32
BF16 = jnp.bfloat16
STEPS = 4
DT = 0.02
N = 128
H = 16
E = 40
FORCE_ROWS = ((12, 0), (8, 12), (4, 20))
VMEM_LIMIT = 28 * 1024 * 1024


def gll():
    inner = math.sqrt(3.0 / 7.0)
    x = np.array([-1.0, -inner, 0.0, inner, 1.0])
    w = np.array([0.1, 49.0 / 90.0, 32.0 / 45.0, 49.0 / 90.0, 0.1])
    leg = (35.0 * x**4 - 30.0 * x**2 + 3.0) / 8.0
    d = np.zeros((5, 5))
    for i in range(5):
        for j in range(5):
            if i != j:
                d[i, j] = leg[i] / (leg[j] * (x[i] - x[j]))
    d[0, 0] = -5.0
    d[4, 4] = 5.0
    return d, w


DER, W = gll()
BACK = (DER * W[:, None]).T
PERIODIC = [2 * W[0], W[1], W[2], W[3]]


def apply5(m, v):
    s0, s1, m0, m1 = v[0] + v[4], v[1] + v[3], v[0] - v[4], v[1] - v[3]
    f = lambda a: float(np.float32(a))
    out = [None] * 5
    for i in (0, 1):
        p = f((m[i, 0] - m[i, 4]) / 2) * m0 + f((m[i, 1] - m[i, 3]) / 2) * m1
        q = f((m[i, 0] + m[i, 4]) / 2) * s0 + f((m[i, 1] + m[i, 3]) / 2) * s1 + f(m[i, 2]) * v[2]
        out[i], out[4 - i] = p + q, p - q
    out[2] = f(m[2, 0]) * m0 + f(m[2, 1]) * m1
    return out


def column_of(x, comp):
    if 0 <= x < N:
        return x
    return N + 32 * comp + (x - N if x >= N else x + 32)


def east_tables():
    grad = np.zeros((3, 256, 256))
    sel = np.zeros((256, 256))
    weight = np.zeros((1, 256))
    for k in range(E):
        for i in range(5):
            q = i * E + k
            xi = 4 * (k - 4) + i
            weight[0, q] = 0.5 * W[i]
            if xi < N + H:
                sel[column_of(xi, 0), q] = 1.0
            for comp in range(3):
                for j in range(5):
                    xj = 4 * (k - 4) + j
                    if xj < N + H:
                        grad[comp, column_of(xj, comp), q] = DER[i, j]

    def two(a):
        hi = a.astype(np.float32).astype(jnp.bfloat16)
        lo = (a - hi.astype(np.float64)).astype(np.float32).astype(jnp.bfloat16)
        return np.stack([hi, lo], axis=1)

    back = np.ascontiguousarray(np.swapaxes(grad, 1, 2))
    return two(grad), two(back), sel.astype(jnp.bfloat16), weight.astype(np.float32)


def shifted(block, axis, distance):
    n = lax.axis_size(axis)
    return lax.ppermute(block, axis, [((i - distance) % n, i) for i in range(n)])


def in_hbm(*arrays):
    return [pltpu.with_memory_space_constraint(x, pltpu.HBM) for x in arrays]


def dot(a, b):
    return jnp.dot(a, b, preferred_element_type=F32)


def split2(x):
    hi = x.astype(BF16)
    return hi, (x - hi.astype(F32)).astype(BF16)


def lane_ids(shape):
    return lax.broadcasted_iota(jnp.int32, shape, len(shape) - 1)


def east_weight(shape):
    r = lane_ids(shape) % 4
    f = lambda a: float(np.float32(a))
    return jnp.where(r == 0, f(PERIODIC[0]), jnp.where(r == 2, f(PERIODIC[2]), f(PERIODIC[1])))


def lane_move(x, shift, start, width=16):
    shift %= 128
    y = pltpu.roll(x, shift, x.ndim - 1) if shift else x
    lane = lane_ids(x.shape)
    return jnp.where((lane >= start) & (lane < start + width), y, 0.0)


WEST_GROUPS = ((0, 12, 116, 0), (12, 8, 120, 1), (20, 4, 124, 2))
EAST_GROUPS = ((24, 9, 0, 0), (33, 5, 0, 1), (38, 1, 0, 2))


def begin_kernel(
    d_ref, v_ref, m_ref, r_ref, tr_ref, id_ref,
    west_ref, east_ref, north_ref, south_ref, ln_ref, ls_ref, sent_ref,
    buf, west_buf, east_buf, tr_buf, sent_buf, id_buf, in_sem, row_sem, out_sem, tr_sem, sent_sem,
):
    copy = pltpu.make_async_copy
    loads = []
    for z in range(5):
        loads.append(
            [
                copy(d_ref.at[:, z], buf.at[z, 0:3], in_sem.at[z, 0]),
                copy(v_ref.at[:, z], buf.at[z, 3:6], in_sem.at[z, 1]),
                copy(m_ref.at[z], buf.at[z, 6], in_sem.at[z, 2]),
                copy(r_ref.at[z], buf.at[z, 7], in_sem.at[z, 3]),
            ]
        )
        for c in loads[z]:
            c.start()
    records = []
    for g in range(8):
        at = pl.ds(64 * g, 64)
        records.append(copy(tr_ref.at[:, at], tr_buf.at[:, at], tr_sem.at[g]))
        records[g].start()
    mine = lane_ids((N, 4 * N)) // STEPS == lax.broadcasted_iota(jnp.int32, (N, 4 * N), 0)
    spread = jnp.where(mine, jnp.broadcast_to(id_ref[...].astype(F32), (N, 4 * N)), 0.0).astype(BF16)
    step = lax.broadcasted_iota(jnp.int32, (4 * N, N), 0) % STEPS == lane_ids((4 * N, N))
    id_buf[...] = dot(spread, jnp.where(step, 1.0, 0.0).astype(BF16))
    lane = lane_ids((N, N))
    stores = []
    for z in range(5):
        for c in loads[z]:
            c.wait()
        for i, (at, top, low) in enumerate(
            ((slice(0, 6), north_ref, south_ref), (slice(6, 8), ln_ref, ls_ref))
        ):
            stores.append(copy(buf.at[z, at, N - H : N], top.at[:, z], row_sem.at[z, 2 * i]))
            stores.append(copy(buf.at[z, at, 0:H], low.at[:, z], row_sem.at[z, 2 * i + 1]))
        for c in stores[-4:]:
            c.start()
        west = buf[z, 0]
        east = pltpu.roll(west, N - 112, 1)
        for a in range(1, 8):
            x = buf[z, a]
            west = jnp.where(lane < 16 * a, west, pltpu.roll(x, 16 * a, 1))
            east = jnp.where(
                lane < 16 * a, east, pltpu.roll(x, (16 * a - 112) % N, 1) if a != 7 else x
            )
        west_buf[z] = west
        east_buf[z] = east
        stores.append(copy(west_buf.at[z], west_ref.at[z], out_sem.at[z, 0]))
        stores.append(copy(east_buf.at[z], east_ref.at[z], out_sem.at[z, 1]))
        for c in stores[-2:]:
            c.start()
    lane = lane_ids((16, N))
    for g in range(8):
        records[g].wait()
        first = 640 * g
        for d in range(16):
            for k in range(9):
                sent_buf[pl.ds(first + 40 * d + 4 * k, 4), :] = tr_buf[k, pl.ds(64 * g + 4 * d, 4), :]
        ids = id_buf[16 * g : 16 * g + 16, :]
        ids = (
            ids
            + pltpu.roll(pltpu.roll(ids, 1, 0), 4, 1)
            + pltpu.roll(pltpu.roll(ids, 15, 0), 8, 1)
        )
        extra = [ids]
        for rho in range(3):
            sides = [jnp.zeros((16, N), F32)] * 2
            for c in range(3):
                for t in range(3):
                    x = tr_buf[3 * rho + c, pl.ds(64 * g + t, 16, stride=4), :]
                    for i, groups in enumerate((WEST_GROUPS, EAST_GROUPS)):
                        off, width, col, _ = groups[t]
                        at = 40 * c + off
                        y = pltpu.roll(x, (at - col) % N, 1) if (at - col) % N else x
                        sides[i] = jnp.where((lane >= at) & (lane < at + width), y, sides[i])
            extra.append(pltpu.roll(sides[0], 1, 0) + pltpu.roll(sides[1], 15, 0))
        for i, x in enumerate(extra):
            for h in range(2):
                sent_buf[pl.ds(first + 320 * h + 36 + i, 8, stride=40), :] = x[8 * h : 8 * h + 8]
        at = pl.ds(first, 640)
        stores.append(copy(sent_buf.at[at], sent_ref.at[at], sent_sem.at[g]))
        stores[-1].start()
    for c in stores:
        c.wait()


def begin(d, v, m, r, records, ids):
    hbm = pl.BlockSpec(memory_space=pltpu.HBM)
    dma = pltpu.SemaphoreType.DMA
    return pl.pallas_call(
        begin_kernel,
        in_specs=[hbm] * 5 + [pl.BlockSpec(memory_space=pltpu.VMEM)],
        out_specs=[hbm] * 7,
        out_shape=[pltpu.HBM((5, N, N), F32)] * 2
        + [pltpu.HBM((6, 5, H, N), F32)] * 2
        + [pltpu.HBM((2, 5, H, N), F32)] * 2
        + [pltpu.HBM((40 * N, N), F32)],
        scratch_shapes=[
            pltpu.VMEM((5, 8, N, N), F32),
            pltpu.VMEM((5, N, N), F32),
            pltpu.VMEM((5, N, N), F32),
            pltpu.VMEM((9, 4 * N, N), F32),
            pltpu.VMEM((40 * N, N), F32),
            pltpu.VMEM((N, N), F32),
            dma((5, 4)),
            dma((5, 4)),
            dma((5, 2)),
            dma((8,)),
            dma((8,)),
        ],
        compiler_params=pltpu.CompilerParams(vmem_limit_bytes=20 * 1024 * 1024),
        name="begin",
    )(*in_hbm(d, v, m, r, records), ids)


def coefs_kernel(m_ref, r_ref, re_ref, rw_ref, out_ref):
    f = lambda a: float(np.float32(a))
    shape = (N, N)
    lane = lane_ids(shape)
    row = lax.broadcasted_iota(jnp.int32, shape, 0) % 4
    pick = lambda n: jnp.where(
        n == 0, f(PERIODIC[0]), jnp.where(n == 2, f(PERIODIC[2]), f(PERIODIC[1]))
    )

    def three(at, mod, rho, ew):
        area = 0.25 * ew * pick(row)
        out_ref[at] = area
        out_ref[at + 1] = area * jnp.sqrt(rho * mod)
        out_ref[at + 2] = area * (0.5 * mod)

    three(0, m_ref[0], r_ref[0], pick(lane % 4))
    mod = rho = jnp.ones(shape, F32)
    node = jnp.zeros(shape, jnp.int32)
    for groups, src, base in ((WEST_GROUPS, rw_ref[0], 112), (EAST_GROUPS, re_ref[0], 0)):
        for c in range(3):
            for off, width, col, _ in groups:
                at = 40 * c + off
                mask = (lane >= at) & (lane < at + width)
                mod = jnp.where(mask, pltpu.roll(src, (at - 96 - (col - base)) % N, 1), mod)
                rho = jnp.where(mask, pltpu.roll(src, (at - 112 - (col - base)) % N, 1), rho)
                node = jnp.where(mask, lane - at, node)
    three(3, mod, rho, pick(node % 4))


def coefs(m, r, re, rw):
    plane = pl.BlockSpec((1, N, N), lambda i: (0, 0, 0))
    return pl.pallas_call(
        coefs_kernel,
        grid=(1,),
        in_specs=[plane] * 4,
        out_specs=pl.BlockSpec((6, N, N), lambda i: (0, 0, 0)),
        out_shape=jax.ShapeDtypeStruct((6, N, N), F32),
        name="coefs",
    )(m, r, re, rw)


def place_kernel(
    arr_ref, co_hbm, b_ref, strip_ref, north_ref, south_ref,
    inj_ref, last_ref, side_ref, vid_ref, ids_ref, co_ref, sem,
):
    to_co = pltpu.make_async_copy(co_hbm, co_ref, sem.at[1])
    to_co.start()
    lane = lane_ids((N, N))
    plane = jnp.where(lane < 4, lane, jnp.where(lane < 8, lane - 4, lane - 5))
    vid_ref[...] = arr_ref[:, 36, :].astype(jnp.int32) + N * plane
    to_scalar = pltpu.make_async_copy(vid_ref, ids_ref, sem.at[0])
    to_scalar.start()
    to_scalar.wait()

    def body(s, carry):
        for t in range(STEPS):
            r = ids_ref[s, t]
            inj_ref[pl.ds(pl.multiple_of(r * 8, 8), 8), :] = arr_ref[s, pl.ds(t, 8, stride=4), :]
            last_ref[pl.ds(r, 1), :] = arr_ref[s, 32 + t : 33 + t, :]
        sides = arr_ref[s, 36:40, :]
        for i in range(2):
            for t in range(3):
                at = pl.multiple_of(ids_ref[s, 4 + 4 * i + t] * 4, 4)
                side_ref[pl.ds(at, 4), :] = sides
        return carry

    lax.fori_loop(0, 128, body, 0, unroll=8)
    to_co.wait()
    lane = lane_ids((8, N))

    def combine(k, carry):
        y = pl.multiple_of(k * 8, 8)
        rows = pl.ds(y, 8)
        co = [co_ref[i, rows, :] for i in range(6)]
        for t in range(STEPS):
            for c in range(3):
                base = (t * N + y) * 8
                inc = inj_ref[pl.ds(base + c, 8, stride=8), :]
                vel = inj_ref[pl.ds(base + 3 + c, 8, stride=8), :]
                if c < 2:
                    dis = inj_ref[pl.ds(base + 6 + c, 8, stride=8), :]
                else:
                    dis = last_ref[pl.ds(t * N + y, 8), :]
                b_ref[t, c, rows, :] = co[0] * inc + co[1] * vel + co[2] * dis
        b = None
        for rho in range(3):
            x = jnp.zeros((8, N), F32)
            for i, groups in enumerate((WEST_GROUPS, EAST_GROUPS)):
                for off, width, _, t in groups:
                    part = side_ref[pl.ds(((3 * i + t) * N + y) * 4 + 1 + rho, 8, stride=4), :]
                    mask = (lane >= off) & (lane < off + width)
                    for c in (1, 2):
                        mask = mask | ((lane >= 40 * c + off) & (lane < 40 * c + off + width))
                    x = jnp.where(mask, part, x)
            b = co[3] * x if b is None else b + co[3 + rho] * x
        for t in range(3):
            out = None
            for c in range(3):
                off, width, col, _ = WEST_GROUPS[t]
                start = 32 * c + 16 + col - 112
                p = lane_move(b, start - 40 * c - off, start, width)
                off, width, _, _ = EAST_GROUPS[t]
                p = p + lane_move(b, 32 * c - 40 * c - off, 32 * c, width)
                out = p if out is None else out + p
            strip_ref[t, rows, :] = out
        return carry

    lax.fori_loop(0, 16, combine, 0)
    for t in range(3):
        n, at = FORCE_ROWS[t]
        for ch in range(4):
            x = b_ref.at[t, ch] if ch < 3 else strip_ref.at[t]
            north_ref[ch, at : at + n] = x[N - n :, :]
            south_ref[ch, at : at + n] = x[:n, :]


def place(arrived, co):
    whole = pl.BlockSpec(memory_space=pltpu.VMEM)
    return pl.pallas_call(
        place_kernel,
        in_specs=[whole, pl.BlockSpec(memory_space=pltpu.HBM)],
        out_specs=[whole] * 4,
        out_shape=[
            jax.ShapeDtypeStruct((STEPS, 3, N, N), F32),
            jax.ShapeDtypeStruct((3, N, N), F32),
            jax.ShapeDtypeStruct((4, 24, N), F32),
            jax.ShapeDtypeStruct((4, 24, N), F32),
        ],
        scratch_shapes=[
            pltpu.VMEM((STEPS * N * 8, N), F32),
            pltpu.VMEM((STEPS * N, N), F32),
            pltpu.VMEM((6 * N * 4, N), F32),
            pltpu.VMEM((N, N), jnp.int32),
            pltpu.SMEM((N, N), jnp.int32),
            pltpu.VMEM((6, N, N), F32),
            pltpu.SemaphoreType.DMA((2,)),
        ],
        compiler_params=pltpu.CompilerParams(vmem_limit_bytes=VMEM_LIMIT),
        name="place",
    )(arrived, *in_hbm(co))


def line_forces(d, k, kn, mn_ref, ce_ref, grad_ref, back_ref, channels, emit):
    live = E if channels == 4 else 32
    rows = 5 * 4 * live

    def north(ch):
        m = ch // 3
        for z in range(5):
            v = [d[ch][z, j] for j in range(4)]
            v.append(pltpu.roll(v[0], E - 1, 0))
            g = apply5(DER, v)
            r = apply5(BACK * W[z], [g[i] * mn_ref[m, z, i] for i in range(5)])
            r[0] = r[0] + pltpu.roll(r[4], 1, 0)
            for j in range(4):
                kn[ch][z, j] = r[j]

    def depth(ch):
        m = ch // 3
        for j in range(4):
            x = [d[ch][z, j, :live] for z in range(5)]
            g = apply5(DER, x)
            r = apply5(BACK * PERIODIC[j], [g[z] * mn_ref[m, z, j, :live] for z in range(5)])
            for z in range(5):
                emit(ch, j, z, x[z], (k[ch][z, j, :live] + kn[ch][z, j, :live]) + r[z])

    sh, sl = split2(d[3][:, :, :live].reshape(rows, N))
    strip = None
    for c in range(3):
        mh, ml = split2(d[c][:, :, :live].reshape(rows, N))
        hi = jnp.concatenate([mh, sh], axis=1)
        lo = jnp.concatenate([ml, sl], axis=1)
        g = dot(hi, grad_ref[c, 0]) + dot(lo, grad_ref[c, 0]) + dot(hi, grad_ref[c, 1])
        fh, fl = split2(g * ce_ref[:, :, :live].reshape(rows, 256))
        f = dot(fh, back_ref[c, 0]) + dot(fl, back_ref[c, 0]) + dot(fh, back_ref[c, 1])
        k[c][:, :, :live] = f[:, :N].reshape(5, 4, live, N)
        if channels == 4:
            strip = f[:, N:] if strip is None else strip + f[:, N:]
        north(c)
        if c:
            depth(c - 1)
    if channels == 4:
        north(3)
        k[3][...] = strip.reshape(5, 4, E, N)
    depth(2)
    if channels == 4:
        depth(3)


def expand(xe, xw, src, step):
    out = None
    for c in range(3):
        p = lane_move(xe, 32 * c - src - step * c, 32 * c)
        p = p + lane_move(xw, 32 * c + 16 - src - step * c, 32 * c + 16)
        out = p if out is None else out + p
    return out


def fields(mod, rho, j, z, put):
    f = lambda a: float(np.float32(a))
    ew = east_weight(mod.shape)
    put("mn", 0.5 * mod * ew)
    put("di", DT / (0.125 * rho * ew * (f(PERIODIC[j]) * f(W[z]))))
    if z == 0:
        area = 0.25 * ew * f(PERIODIC[j])
        put("ai", area * jnp.sqrt(rho * mod))
        put("as", area * (0.5 * mod))


def east_coefs(main, strip, sel, weight):
    x = jnp.concatenate([main, strip], axis=1)
    hi = x.astype(BF16)
    mid, lo = split2(x - hi.astype(F32))
    return (dot(hi, sel) + dot(mid, sel) + dot(lo, sel)) * weight


def strip_density(rho):
    return jnp.where(lane_ids(rho.shape) < 96, rho, 1.0)


def early_kernel(
    d_ref, v_ref, m_ref, r_ref, re_ref, rw_ref, sel_ref, qw_ref,
    d_out, v_out, mn_out, di_out, ce_out, ai_out, as_out,
):
    f = lambda a: float(np.float32(a))
    outs = {"mn": mn_out, "di": di_out, "ai": ai_out, "as": as_out}

    def plane(z):
        for j in range(4):
            own = pl.ds(j, 32, stride=4)
            xe, xw = re_ref[z, own, :], rw_ref[z, own, :]
            vs = [v_ref[c, z, own, :] for c in range(3)] + [expand(xe, xw, 48, 16)]
            ds = [d_ref[c, z, own, :] for c in range(3)] + [expand(xe, xw, 0, 16)]
            for ch in range(4):
                v_out[ch, z, j] = vs[ch]
                d_out[ch, z, j] = ds[ch] + DT * vs[ch]
            mods = [m_ref[z, own, :], expand(xe, xw, 96, 0)]
            rhos = [r_ref[z, own, :], strip_density(expand(xe, xw, 112, 0))]
            for m in range(2):

                def put(name, x):
                    at = (m, j) if name in ("ai", "as") else (m, z, j)
                    outs[name][at] = x

                fields(mods[m], rhos[m], j, z, put)
            weight = qw_ref[...] * (f(W[z]) * f(PERIODIC[j]))
            ce_out[z, j] = east_coefs(mods[0], mods[1], sel_ref[...], weight)

    for z in range(5):
        plane(z)


OWN_SHAPES = ((4, 5, 4, 32, N),) * 2 + ((2, 5, 4, 32, N),) * 2 + ((5, 4, 32, 256),) + ((2, 4, 32, N),) * 2


def early(d, v, m, r, re, rw, sel, qw):
    whole = pl.BlockSpec(memory_space=pltpu.VMEM)
    return pl.pallas_call(
        early_kernel,
        in_specs=[whole] * 8,
        out_specs=[whole] * 7,
        out_shape=[jax.ShapeDtypeStruct(x, F32) for x in OWN_SHAPES],
        compiler_params=pltpu.CompilerParams(vmem_limit_bytes=16 * 1024 * 1024),
        name="early",
    )(d, v, m, r, re, rw, sel, qw)


def prepare_kernel(*refs):
    own, halos, tables, refs = refs[:7], refs[7:11], refs[11:15], refs[15:]
    (d0, d1, d2, d3, v0, v1, v2, v3, mn_ref, di_ref, ce_ref, ai_ref, as_ref), refs = refs[:13], refs[13:]
    (k0, k1, k2, k3, n0, n1, n2, n3), refs = refs[:8], refs[8:]
    buffers, (own_sem, halo_sem) = refs[:8], refs[8:]
    d_ref, v_ref = (d0, d1, d2, d3), (v0, v1, v2, v3)
    copy = pltpu.make_async_copy
    node = pl.ds(0, 32)
    late = [copy(x, y, halo_sem.at[i]) for i, (x, y) in enumerate(zip((*halos, *tables), buffers))]
    moves = []
    for ch in range(4):
        moves.append((own[0].at[ch], d_ref[ch].at[:, :, node]))
        moves.append((own[1].at[ch], v_ref[ch].at[:, :, node]))
    for m in range(2):
        moves.append((own[2].at[m], mn_ref.at[m, :, 0:4, node]))
        moves.append((own[3].at[m], di_ref.at[m, :, :, node]))
    moves.append((own[4], ce_ref.at[:, :, node]))
    moves.append((own[5], ai_ref.at[:, :, node]))
    moves.append((own[6], as_ref.at[:, :, node]))
    moves = [copy(x, y, own_sem.at[i]) for i, (x, y) in enumerate(moves)]
    for c in late + moves:
        c.start()
    n_ref, s_ref, cn_ref, cs_ref, sel_ref, qw_ref, grad_ref, back_ref = buffers
    outs = {"mn": mn_ref, "di": di_ref, "ai": ai_ref, "as": as_ref}
    f = lambda a: float(np.float32(a))
    for c in late:
        c.wait()

    def halo(at, j, north=n_ref, south=s_ref):
        at = (*at, pl.ds(j, 4, stride=4), slice(None))
        return jnp.concatenate([north[at], south[at]], axis=0)

    rest = slice(32, E)
    mains, sides = [], []
    for z in range(5):
        for j in range(4):
            xe, xw, mod, rho = (halo((i, z), j, cn_ref, cs_ref) for i in (2, 3, 0, 1))
            vs = [halo((3 + c, z), j) for c in range(3)] + [expand(xe, xw, 48, 16)]
            ds = [halo((c, z), j) for c in range(3)] + [expand(xe, xw, 0, 16)]
            for ch in range(4):
                v_ref[ch][z, j, rest] = vs[ch]
                d_ref[ch][z, j, rest] = ds[ch] + DT * vs[ch]
            mods = [mod, expand(xe, xw, 96, 0)]
            rhos = [rho, strip_density(expand(xe, xw, 112, 0))]
            for m in range(2):

                def put(name, x):
                    at = (m, j, rest) if name in ("ai", "as") else (m, z, j, rest)
                    outs[name][at] = x

                fields(mods[m], rhos[m], j, z, put)
            mains.append(mods[0])
            sides.append(mods[1])
    c = east_coefs(jnp.concatenate(mains), jnp.concatenate(sides), sel_ref[...], qw_ref[...])
    for z in range(5):
        for j in range(4):
            at = (z * 4 + j) * 8
            ce_ref[z, j, rest] = c[at : at + 8] * (f(W[z]) * f(PERIODIC[j]))
    for c in moves:
        c.wait()
    for m in range(2):
        for z in range(5):
            mn_ref[m, z, 4] = pltpu.roll(mn_ref[m, z, 0], E - 1, 0)

    def emit(ch, j, z, d, k):
        m = ch // 3
        v = v_ref[ch][z, j]
        if z == 0:
            k = k + ai_ref[m, j] * v + as_ref[m, j] * d
        v_ref[ch][z, j] = v - di_ref[m, z, j] * k

    line_forces(
        d_ref, (k0, k1, k2, k3), (n0, n1, n2, n3), mn_ref, ce_ref, grad_ref, back_ref, 4, emit
    )


def prepare(own, halos, tables):
    grad, back, sel, qw = tables
    whole = pl.BlockSpec(memory_space=pltpu.VMEM)
    state = jax.ShapeDtypeStruct((5, 4, E, N), F32)
    late = (*halos, sel, qw, grad, back)
    return pl.pallas_call(
        prepare_kernel,
        in_specs=[pl.BlockSpec(memory_space=pltpu.HBM)] * 15,
        out_specs=[whole] * 13,
        out_shape=[
            *[state] * 8,
            jax.ShapeDtypeStruct((2, 5, 5, E, N), F32),
            jax.ShapeDtypeStruct((2, 5, 4, E, N), F32),
            jax.ShapeDtypeStruct((5, 4, E, 256), F32),
            jax.ShapeDtypeStruct((2, 4, E, N), F32),
            jax.ShapeDtypeStruct((2, 4, E, N), F32),
        ],
        scratch_shapes=[pltpu.VMEM((5, 4, E, N), F32)] * 8
        + [pltpu.VMEM(x.shape, x.dtype) for x in late]
        + [pltpu.SemaphoreType.DMA((15,)), pltpu.SemaphoreType.DMA((8,))],
        compiler_params=pltpu.CompilerParams(vmem_limit_bytes=VMEM_LIMIT),
        name="prepare",
    )(*in_hbm(*own, *late))


def steps_kernel(
    i0, i1, i2, i3, u0, u1, u2, u3, mn_ref, di_ref, ce_ref, ai_ref, as_ref,
    b_ref, bs_ref, bn_ref, bo_ref, grad_ref, back_ref,
    dout_ref, vout_ref,
    d0, d1, d2, d3, v0, v1, v2, v3, k0, k1, k2, k3, n0, n1, n2, n3, f_ref,
):
    d_in, v_in = (i0, i1, i2, i3), (u0, u1, u2, u3)
    d_ref, v_ref = (d0, d1, d2, d3), (v0, v1, v2, v3)
    k_ref, kn_ref = (k0, k1, k2, k3), (n0, n1, n2, n3)
    for t in range(3):
        n, at = FORCE_ROWS[t]
        gap = jnp.zeros((8 - n // 2, N), F32)
        for ch in range(4):
            for j in range(4):
                own = pl.ds(j, 32, stride=4)
                x = b_ref[t, ch, own, :] if ch < 3 else bs_ref[t, own, :]
                halo = pl.ds(at + j, n // 4, stride=4)
                f_ref[t, ch, j] = jnp.concatenate(
                    [x, bn_ref[ch, halo, :], gap, bo_ref[ch, halo, :]], axis=0
                )
    for ch in range(3):
        for j in range(4):
            x = b_ref[3, ch, pl.ds(j, 32, stride=4), :]
            f_ref[3, ch, j] = jnp.concatenate([x, jnp.zeros((8, N), F32)], axis=0)

    for ch in range(4):
        for j in range(4):
            for z in range(5):
                v = v_in[ch][z, j]
                if z == 0:
                    v = v + di_ref[ch // 3, z, j] * f_ref[0, ch, j]
                v_ref[ch][z, j] = v
                d_ref[ch][z, j] = d_in[ch][z, j] + DT * v

    def velocity(t, ch, j, z, d, k):
        m = ch // 3
        n = slice(0, d.shape[0])
        v = v_ref[ch][z, j, n]
        if z == 0:
            k = k + ai_ref[m, j, n] * v + as_ref[m, j, n] * d - f_ref[t, ch, j, n]
        return v - di_ref[m, z, j, n] * k

    def step(t, carry):
        def emit(ch, j, z, d, k):
            v = velocity(t, ch, j, z, d, k)
            v_ref[ch][z, j] = v
            d_ref[ch][z, j] = d + DT * v

        line_forces(d_ref, k_ref, kn_ref, mn_ref, ce_ref, grad_ref, back_ref, 4, emit)
        return carry

    lax.fori_loop(1, 3, step, 0)

    def final(ch, j, z, d, k):
        dout_ref[ch, z, pl.ds(j, 32, stride=4), :] = d
        vout_ref[ch, z, pl.ds(j, 32, stride=4), :] = velocity(3, ch, j, z, d, k)

    line_forces(d_ref, k_ref, kn_ref, mn_ref, ce_ref, grad_ref, back_ref, 3, final)


def steps(prepared, b, bs, bn, bo, tables):
    grad, back = tables[:2]
    whole = pl.BlockSpec(memory_space=pltpu.VMEM)
    return pl.pallas_call(
        steps_kernel,
        in_specs=[whole] * 19,
        out_specs=[whole] * 2,
        out_shape=[jax.ShapeDtypeStruct((3, 5, N, N), F32)] * 2,
        scratch_shapes=[pltpu.VMEM((5, 4, E, N), F32)] * 16 + [pltpu.VMEM((4, 4, 4, E, N), F32)],
        compiler_params=pltpu.CompilerParams(vmem_limit_bytes=VMEM_LIMIT),
        name="steps",
    )(*prepared, b, bs, bn, bo, grad, back)


def local(displacement, velocity, modulus, density, traces, record_row):
    tables = tuple(jnp.asarray(t) for t in east_tables())
    west, east, north, south, late_north, late_south, sent = begin(
        displacement, velocity, modulus, density, jnp.transpose(traces[0], (1, 0, 2)), record_row
    )
    from_east = shifted(west, "reg", -1)
    from_west = shifted(east, "reg", 1)
    from_north = shifted(south, "src", -1)
    from_south = shifted(north, "src", 1)
    arrived = lax.all_to_all(
        sent.reshape(N, 40, N), ("src", "reg"), split_axis=0, concat_axis=0, tiled=True
    )
    corner = jnp.stack([from_east, from_west])
    late_south = jnp.concatenate([late_south, corner[:, :, :H]], axis=0)
    late_north = jnp.concatenate([late_north, corner[:, :, N - H :]], axis=0)
    corner_north = shifted(late_south, "src", -1)
    corner_south = shifted(late_north, "src", 1)
    co = coefs(modulus, density, from_east, from_west)
    own = early(displacement, velocity, modulus, density, from_east, from_west, *tables[2:])
    b, b_strip, b_north, b_south = place(arrived, co)
    b_from_south = shifted(b_north, "src", 1)
    b_from_north = shifted(b_south, "src", -1)
    from_north, from_south, corner_north, corner_south, _ = lax.optimization_barrier(
        (from_north, from_south, corner_north, corner_south, b)
    )
    prepared = prepare(own, (from_north, from_south, corner_north, corner_south), tables)
    return steps(prepared, b, b_strip, b_from_north, b_from_south, tables)


def solution(mesh):
    state = P(None, None, "src", "reg")
    field = P(None, "src", "reg")
    in_specs = (state, state, field, field, P(("src", "reg"), None, None, None), P(("src", "reg"), None))
    return jax.shard_map(local, mesh=mesh, in_specs=in_specs, out_specs=(state, state), check_vma=False)
```

```python
import math

import jax
import jax.numpy as jnp
import numpy as np
from jax import lax
from jax.experimental import pallas as pl
from jax.experimental.pallas import tpu as pltpu
from jax.sharding import PartitionSpec as P


F32 = jnp.float32
BF16 = jnp.bfloat16
STEPS = 4
DT = 0.02
N = 128
H = 16
E = 40
FORCE_ROWS = ((12, 0), (8, 12), (4, 20))
VMEM_LIMIT = 28 * 1024 * 1024


def gll():
    inner = math.sqrt(3.0 / 7.0)
    x = np.array([-1.0, -inner, 0.0, inner, 1.0])
    w = np.array([0.1, 49.0 / 90.0, 32.0 / 45.0, 49.0 / 90.0, 0.1])
    leg = (35.0 * x**4 - 30.0 * x**2 + 3.0) / 8.0
    d = np.zeros((5, 5))
    for i in range(5):
        for j in range(5):
            if i != j:
                d[i, j] = leg[i] / (leg[j] * (x[i] - x[j]))
    d[0, 0] = -5.0
    d[4, 4] = 5.0
    return d, w


DER, W = gll()
PERIODIC = [2 * W[0], W[1], W[2], W[3]]


def network():
    odd = [[(DER[i, 0] - DER[i, 4]) / 2, (DER[i, 1] - DER[i, 3]) / 2] for i in (0, 1)]
    even = [[(DER[i, 0] + DER[i, 4]) / 2, (DER[i, 1] + DER[i, 3]) / 2] for i in (0, 1)]
    scale = [even[0][0], even[1][0], DER[2, 0]]
    f = lambda x: float(np.float32(x))
    p = [[f(odd[i][k] / scale[i]) for k in range(2)] for i in range(2)]
    q = [f(even[i][1] / scale[i]) for i in range(2)]
    scale = np.array(scale + scale[1::-1])
    return p, q, f(DER[2, 1] / DER[2, 0]), W * scale**2


ODD, EVEN, MIDDLE, POINT = network()


def slopes(v):
    twice = v[2] + v[2]
    u0, u1 = (v[0] + v[4]) - twice, (v[1] + v[3]) - twice
    m0, m1 = v[0] - v[4], v[1] - v[3]
    out = [None] * 5
    for i in (0, 1):
        p = ODD[i][0] * m0 + ODD[i][1] * m1
        q = u0 + EVEN[i] * u1
        out[i], out[4 - i] = p + q, p - q
    out[2] = m0 + MIDDLE * m1
    return out


def tested(f):
    ep, eq = [f[0] + f[4], f[1] + f[3]], [f[0] - f[4], f[1] - f[3]]
    m0 = (ODD[0][0] * ep[0] + ODD[1][0] * ep[1]) + f[2]
    m1 = (ODD[0][1] * ep[0] + ODD[1][1] * ep[1]) + MIDDLE * f[2]
    u0 = eq[0] + eq[1]
    u1 = EVEN[0] * eq[0] + EVEN[1] * eq[1]
    return [u0 + m0, u1 + m1, -2.0 * (u0 + u1), u1 - m1, u0 - m0]


def column_of(x, comp):
    if 0 <= x < N:
        return x
    return N + 32 * comp + (x - N if x >= N else x + 32)


def east_tables():
    grad = np.zeros((3, 256, 256))
    sel = np.zeros((256, 256))
    weight = np.zeros((1, 256))
    for k in range(E):
        for i in range(5):
            q = i * E + k
            xi = 4 * (k - 4) + i
            weight[0, q] = 0.5 * W[i]
            if xi < N + H:
                sel[column_of(xi, 0), q] = 1.0
            for comp in range(3):
                for j in range(5):
                    xj = 4 * (k - 4) + j
                    if xj < N + H:
                        grad[comp, column_of(xj, comp), q] = DER[i, j]

    def two(a):
        hi = a.astype(np.float32).astype(jnp.bfloat16)
        lo = (a - hi.astype(np.float64)).astype(np.float32).astype(jnp.bfloat16)
        return np.stack([hi, lo], axis=1)

    back = np.ascontiguousarray(np.swapaxes(grad, 1, 2))
    return two(grad), two(back), sel.astype(jnp.bfloat16), weight.astype(np.float32)


def shifted(block, axis, distance):
    n = lax.axis_size(axis)
    return lax.ppermute(block, axis, [((i - distance) % n, i) for i in range(n)])


def in_hbm(*arrays):
    return [pltpu.with_memory_space_constraint(x, pltpu.HBM) for x in arrays]


def dot(a, b):
    return jnp.dot(a, b, preferred_element_type=F32)


def split2(x):
    hi = x.astype(BF16)
    return hi, (x - hi.astype(F32)).astype(BF16)


def lane_ids(shape):
    return lax.broadcasted_iota(jnp.int32, shape, len(shape) - 1)


def east_weight(shape):
    r = lane_ids(shape) % 4
    f = lambda a: float(np.float32(a))
    return jnp.where(r == 0, f(PERIODIC[0]), jnp.where(r == 2, f(PERIODIC[2]), f(PERIODIC[1])))


def moved(x, shift):
    return pltpu.roll(x, shift % N, x.ndim - 1) if shift % N else x


def lane_move(x, shift, start, width=16):
    shift %= 128
    y = pltpu.roll(x, shift, x.ndim - 1) if shift else x
    lane = lane_ids(x.shape)
    return jnp.where((lane >= start) & (lane < start + width), y, 0.0)


WEST_GROUPS = ((0, 12, 116, 0), (21, 8, 120, 1), (34, 4, 124, 2))
EAST_GROUPS = ((12, 9, 0, 0), (29, 5, 0, 1), (38, 1, 0, 2))
TO_WEST = (0, 32, 64, 96, 16, 48, 80, 112)
TO_EAST = (112, 16, 48, 80, 0, 32, 64, 96)


def begin_kernel(
    d_ref, v_ref, m_ref, r_ref, tr_ref, id_ref,
    west_ref, east_ref, north_ref, south_ref, ln_ref, ls_ref, sent_ref,
    buf, west_buf, east_buf, tr_buf, sent_buf, id_buf, row_buf, in_sem, row_sem, out_sem, tr_sem, sent_sem,
):
    copy = pltpu.make_async_copy
    face_rows = copy(id_ref, row_buf, sent_sem.at[8])
    face_rows.start()
    loads = []
    for z in range(5):
        loads.append(
            [
                copy(d_ref.at[:, z], buf.at[z, 0:3], in_sem.at[z, 0]),
                copy(v_ref.at[:, z], buf.at[z, 3:6], in_sem.at[z, 1]),
                copy(m_ref.at[z], buf.at[z, 6], in_sem.at[z, 2]),
                copy(r_ref.at[z], buf.at[z, 7], in_sem.at[z, 3]),
            ]
        )
        for c in loads[z]:
            c.start()
    records = []
    for g in range(8):
        at = pl.ds(64 * g, 64)
        records.append(copy(tr_ref.at[:, at], tr_buf.at[:, at], tr_sem.at[g]))
        records[g].start()
    lane = lane_ids((N, N))
    stores = []
    for z in range(5):
        for c in loads[z]:
            c.wait()
        for i, (at, top, low) in enumerate(
            ((slice(0, 6), north_ref, south_ref), (slice(6, 8), ln_ref, ls_ref))
        ):
            stores.append(copy(buf.at[z, at, N - H : N], top.at[:, z], row_sem.at[z, 2 * i]))
            stores.append(copy(buf.at[z, at, 0:H], low.at[:, z], row_sem.at[z, 2 * i + 1]))
        for c in stores[-4:]:
            c.start()
        packed = []
        for h in range(2):
            x = buf[z, 4 * h]
            for a in range(1, 4):
                mask = (lane >= 32 * a - 16) & (lane < 32 * a + 16)
                x = jnp.where(mask, pltpu.roll(buf[z, 4 * h + a], 32 * a, 1), x)
            packed.append(x)
        other = pltpu.roll(packed[1], 16, 1)
        west_buf[z] = jnp.where(lane % 32 < 16, packed[0], other)
        east_buf[z] = jnp.where(lane % 32 < 16, other, packed[0])
        stores.append(copy(west_buf.at[z], west_ref.at[z], out_sem.at[z, 0]))
        stores.append(copy(east_buf.at[z], east_ref.at[z], out_sem.at[z, 1]))
        for c in stores[-2:]:
            c.start()
    face_rows.wait()
    mine = lane_ids((N, 4 * N)) // STEPS == lax.broadcasted_iota(jnp.int32, (N, 4 * N), 0)
    spread = jnp.where(mine, jnp.broadcast_to(row_buf[...].astype(F32), (N, 4 * N)), 0.0).astype(BF16)
    step = lax.broadcasted_iota(jnp.int32, (4 * N, N), 0) % STEPS == lane_ids((4 * N, N))
    id_buf[...] = dot(spread, jnp.where(step, 1.0, 0.0).astype(BF16))
    lane = lane_ids((16, N))
    for g in range(8):
        records[g].wait()
        first = 640 * g
        for d in range(16):
            for k in range(9):
                sent_buf[pl.ds(first + 40 * d + 4 * k, 4), :] = tr_buf[k, pl.ds(64 * g + 4 * d, 4), :]
        ids = id_buf[16 * g : 16 * g + 16, :]
        ids = (
            ids
            + pltpu.roll(pltpu.roll(ids, 1, 0), 4, 1)
            + pltpu.roll(pltpu.roll(ids, 15, 0), 8, 1)
        )
        extra = [ids]
        for rho in range(3):
            sides = [jnp.zeros((16, N), F32)] * 2
            for c in range(3):
                for t in range(3):
                    x = tr_buf[3 * rho + c, pl.ds(64 * g + t, 16, stride=4), :]
                    for i, groups in enumerate((WEST_GROUPS, EAST_GROUPS)):
                        off, width, col, _ = groups[t]
                        at = 40 * c + off
                        y = pltpu.roll(x, (at - col) % N, 1) if (at - col) % N else x
                        sides[i] = jnp.where((lane >= at) & (lane < at + width), y, sides[i])
            extra.append(pltpu.roll(sides[0], 1, 0) + pltpu.roll(sides[1], 15, 0))
        for i, x in enumerate(extra):
            for h in range(2):
                sent_buf[pl.ds(first + 320 * h + 36 + i, 8, stride=40), :] = x[8 * h : 8 * h + 8]
        at = pl.ds(first, 640)
        stores.append(copy(sent_buf.at[at], sent_ref.at[at], sent_sem.at[g]))
        stores[-1].start()
    for c in stores:
        c.wait()


def begin(d, v, m, r, records, ids):
    hbm = pl.BlockSpec(memory_space=pltpu.HBM)
    dma = pltpu.SemaphoreType.DMA
    return pl.pallas_call(
        begin_kernel,
        in_specs=[hbm] * 6,
        out_specs=[hbm] * 7,
        out_shape=[pltpu.HBM((5, N, N), F32)] * 2
        + [pltpu.HBM((6, 5, H, N), F32)] * 2
        + [pltpu.HBM((2, 5, H, N), F32)] * 2
        + [pltpu.HBM((40 * N, N), F32)],
        scratch_shapes=[
            pltpu.VMEM((5, 8, N, N), F32),
            pltpu.VMEM((5, N, N), F32),
            pltpu.VMEM((5, N, N), F32),
            pltpu.VMEM((9, 4 * N, N), F32),
            pltpu.VMEM((40 * N, N), F32),
            pltpu.VMEM((N, N), F32),
            pltpu.VMEM((1, STEPS * N), jnp.int32),
            dma((5, 4)),
            dma((5, 4)),
            dma((5, 2)),
            dma((8,)),
            dma((9,)),
        ],
        compiler_params=pltpu.CompilerParams(vmem_limit_bytes=20 * 1024 * 1024),
        name="begin",
    )(*in_hbm(d, v, m, r, records, ids))


def coefs_kernel(m_ref, r_ref, re_ref, rw_ref, out_ref):
    f = lambda a: float(np.float32(a))
    shape = (N, N)
    lane = lane_ids(shape)
    row = lax.broadcasted_iota(jnp.int32, shape, 0) % 4
    pick = lambda n: jnp.where(
        n == 0, f(PERIODIC[0]), jnp.where(n == 2, f(PERIODIC[2]), f(PERIODIC[1]))
    )

    def three(at, mod, rho, ew):
        area = 0.25 * ew * pick(row)
        out_ref[at] = area
        out_ref[at + 1] = area * jnp.sqrt(rho * mod)
        out_ref[at + 2] = area * (0.5 * mod)

    three(0, m_ref[0], r_ref[0], pick(lane % 4))
    mod = rho = jnp.ones(shape, F32)
    node = jnp.zeros(shape, jnp.int32)
    for groups, src, base, at_lane in (
        (WEST_GROUPS, rw_ref[0], 112, TO_EAST),
        (EAST_GROUPS, re_ref[0], 0, TO_WEST),
    ):
        for c in range(3):
            for off, width, col, _ in groups:
                at = 40 * c + off
                mask = (lane >= at) & (lane < at + width)
                mod = jnp.where(mask, moved(src, at - at_lane[6] - (col - base)), mod)
                rho = jnp.where(mask, moved(src, at - at_lane[7] - (col - base)), rho)
                node = jnp.where(mask, lane - at, node)
    three(3, mod, rho, pick(node % 4))


def coefs(m, r, re, rw):
    plane = pl.BlockSpec((1, N, N), lambda i: (0, 0, 0))
    return pl.pallas_call(
        coefs_kernel,
        grid=(1,),
        in_specs=[plane] * 4,
        out_specs=pl.BlockSpec((6, N, N), lambda i: (0, 0, 0)),
        out_shape=jax.ShapeDtypeStruct((6, N, N), F32),
        name="coefs",
    )(m, r, re, rw)


def place_kernel(*refs):
    (arr_ref, co_hbm), own, refs = refs[:2], refs[2:10], refs[10:]
    (b_ref, strip_ref, north_ref, south_ref), fetched, refs = refs[:4], refs[4:18], refs[18:]
    inj_ref, side_ref, vid_ref, ids_ref, co_ref, sem, own_sem = refs
    copy = pltpu.make_async_copy
    lane = lane_ids((N, N))
    plane = jnp.where(lane < 8, lane % 4, lane - 5)
    slot = jnp.where(lane < 4, 16, 8)
    where_to = (arr_ref[:, 36, :].astype(jnp.int32) + N * plane) * slot
    vid_ref[...] = jnp.transpose(where_to)[:16]
    to_scalar = copy(vid_ref, ids_ref, sem.at[0])
    to_scalar.start()
    to_co = copy(co_hbm, co_ref, sem.at[1])
    to_co.start()
    node = pl.ds(0, 32)
    moves = []
    for ch in range(4):
        moves.append((own[0].at[ch], fetched[ch].at[:, :, node]))
        moves.append((own[1].at[ch], fetched[4 + ch].at[:, :, node]))
    for m in range(2):
        moves.append((own[2].at[m], fetched[8].at[m, :, 0:4, node]))
        moves.append((own[3].at[m], fetched[9].at[m, :, :, node]))
        moves.append((own[4].at[m], fetched[10].at[m, :, :, node]))
    for i in (5, 6, 7):
        moves.append((own[i], fetched[6 + i].at[:, :, node]))
    moves = [copy(x, y, own_sem.at[i]) for i, (x, y) in enumerate(moves)]
    to_scalar.wait()
    for c in moves:
        c.start()

    def body(s, carry):
        tail = arr_ref[s, 32:40, :]
        for t in range(STEPS):
            at = pl.multiple_of(ids_ref[t, s], 16)
            inj_ref[pl.ds(at, 8), :] = arr_ref[s, pl.ds(t, 8, stride=4), :]
            inj_ref[pl.ds(at + 8, 8), :] = tail
        for i in range(2):
            for t in range(3):
                side_ref[pl.ds(pl.multiple_of(ids_ref[4 + 4 * i + t, s], 8), 8), :] = tail
        return carry

    lax.fori_loop(0, 128, body, 0, unroll=8)
    to_co.wait()
    lane = lane_ids((8, N))

    def combine(k, carry):
        y = pl.multiple_of(k * 8, 8)
        rows = pl.ds(y, 8)
        co = [co_ref[i, rows, :] for i in range(6)]
        for t in range(STEPS):
            for c in range(3):
                base = (t * N + y) * 16
                inc = inj_ref[pl.ds(base + c, 8, stride=16), :]
                vel = inj_ref[pl.ds(base + 3 + c, 8, stride=16), :]
                dis = inj_ref[pl.ds(base + (6 + c if c < 2 else 8 + t), 8, stride=16), :]
                b_ref[t, c, rows, :] = co[0] * inc + co[1] * vel + co[2] * dis
        b = None
        for rho in range(3):
            x = jnp.zeros((8, N), F32)
            for i, groups in enumerate((WEST_GROUPS, EAST_GROUPS)):
                for off, width, _, t in groups:
                    part = side_ref[pl.ds(((3 * i + t) * N + y) * 8 + 5 + rho, 8, stride=8), :]
                    mask = (lane >= off) & (lane < off + width)
                    for c in (1, 2):
                        mask = mask | ((lane >= 40 * c + off) & (lane < 40 * c + off + width))
                    x = jnp.where(mask, part, x)
            b = co[3] * x if b is None else b + co[3 + rho] * x
        for t in range(3):
            out = None
            for c in range(3):
                off, width, col, _ = WEST_GROUPS[t]
                start = 32 * c + 16 + col - 112
                p = lane_move(b, start - 40 * c - off, start, width)
                off, width, _, _ = EAST_GROUPS[t]
                p = p + lane_move(b, 32 * c - 40 * c - off, 32 * c, width)
                out = p if out is None else out + p
            strip_ref[t, rows, :] = out
        return carry

    lax.fori_loop(0, 16, combine, 0)
    for t in range(3):
        n, at = FORCE_ROWS[t]
        for ch in range(4):
            x = b_ref.at[t, ch] if ch < 3 else strip_ref.at[t]
            north_ref[ch, at : at + n] = x[N - n :, :]
            south_ref[ch, at : at + n] = x[:n, :]
    for c in moves:
        c.wait()


PREPARED = (
    *[jax.ShapeDtypeStruct((5, 4, E, N), F32)] * 8,
    jax.ShapeDtypeStruct((2, 5, 5, E, N), F32),
    jax.ShapeDtypeStruct((2, 5, 4, E, N), F32),
    jax.ShapeDtypeStruct((2, 5, 4, E, N), F32),
    jax.ShapeDtypeStruct((5, 4, E, 256), F32),
    jax.ShapeDtypeStruct((2, 4, E, N), F32),
    jax.ShapeDtypeStruct((2, 4, E, N), F32),
)


def place(arrived, co, own):
    whole = pl.BlockSpec(memory_space=pltpu.VMEM)
    return pl.pallas_call(
        place_kernel,
        in_specs=[whole] + [pl.BlockSpec(memory_space=pltpu.HBM)] * 9,
        out_specs=[whole] * 18,
        out_shape=[
            jax.ShapeDtypeStruct((STEPS, 3, N, N), F32),
            jax.ShapeDtypeStruct((3, N, N), F32),
            jax.ShapeDtypeStruct((4, 24, N), F32),
            jax.ShapeDtypeStruct((4, 24, N), F32),
            *PREPARED,
        ],
        scratch_shapes=[
            pltpu.VMEM((STEPS * N * 16, N), F32),
            pltpu.VMEM((6 * N * 8, N), F32),
            pltpu.VMEM((16, N), jnp.int32),
            pltpu.SMEM((16, N), jnp.int32),
            pltpu.VMEM((6, N, N), F32),
            pltpu.SemaphoreType.DMA((2,)),
            pltpu.SemaphoreType.DMA((17,)),
        ],
        compiler_params=pltpu.CompilerParams(vmem_limit_bytes=VMEM_LIMIT),
        name="place",
    )(arrived, *in_hbm(co, *own))


def line_forces(d, k, kn, mn_ref, md_ref, ce_ref, grad_ref, back_ref, channels, emit):
    live = E if channels == 4 else 32
    rows = 5 * 4 * live

    def north(ch):
        m = ch // 3
        for z in range(5):
            v = [d[ch][z, j] for j in range(4)]
            v.append(pltpu.roll(v[0], E - 1, 0))
            g = slopes(v)
            r = tested([g[i] * mn_ref[m, z, i] for i in range(5)])
            r[0] = r[0] + pltpu.roll(r[4], 1, 0)
            for j in range(4):
                kn[ch][z, j] = r[j]

    def depth(ch):
        m = ch // 3
        for j in range(4):
            x = [d[ch][z, j, :live] for z in range(5)]
            g = slopes(x)
            r = tested([g[z] * md_ref[m, z, j, :live] for z in range(5)])
            for z in range(5):
                emit(ch, j, z, x[z], (k[ch][z, j, :live] + kn[ch][z, j, :live]) + r[z])

    sh, sl = split2(d[3][:, :, :live].reshape(rows, N))
    strip = None
    for c in range(3):
        mh, ml = split2(d[c][:, :, :live].reshape(rows, N))
        hi = jnp.concatenate([mh, sh], axis=1)
        lo = jnp.concatenate([ml, sl], axis=1)
        g = dot(hi, grad_ref[c, 0]) + dot(lo, grad_ref[c, 0]) + dot(hi, grad_ref[c, 1])
        fh, fl = split2(g * ce_ref[:, :, :live].reshape(rows, 256))
        f = dot(fh, back_ref[c, 0]) + dot(fl, back_ref[c, 0]) + dot(fh, back_ref[c, 1])
        k[c][:, :, :live] = f[:, :N].reshape(5, 4, live, N)
        if channels == 4:
            strip = f[:, N:] if strip is None else strip + f[:, N:]
        north(c)
        if c:
            depth(c - 1)
    if channels == 4:
        north(3)
        k[3][...] = strip.reshape(5, 4, E, N)
    depth(2)
    if channels == 4:
        depth(3)


def expand(xe, xw, first, step):
    out = None
    for c in range(3):
        p = lane_move(xe, 32 * c - TO_WEST[first + step * c], 32 * c)
        p = p + lane_move(xw, 32 * c + 16 - TO_EAST[first + step * c], 32 * c + 16)
        out = p if out is None else out + p
    return out


def fields(mod, rho, j, z, put):
    f = lambda a: float(np.float32(a))
    ew = east_weight(mod.shape)
    half = 0.5 * mod * ew
    put("mn", half * f(POINT[j] * W[z]))
    put("md", half * f(POINT[z] * PERIODIC[j]))
    put("di", DT / (0.125 * rho * ew * (f(PERIODIC[j]) * f(W[z]))))
    if z == 0:
        area = 0.25 * ew * f(PERIODIC[j])
        put("ai", area * jnp.sqrt(rho * mod))
        put("as", area * (0.5 * mod))


def east_coefs(main, strip, sel, weight):
    x = jnp.concatenate([main, strip], axis=1)
    hi = x.astype(BF16)
    mid, lo = split2(x - hi.astype(F32))
    return (dot(hi, sel) + dot(mid, sel) + dot(lo, sel)) * weight


def strip_density(rho):
    return jnp.where(lane_ids(rho.shape) < 96, rho, 1.0)


def early_kernel(
    d_ref, v_ref, m_ref, r_ref, re_ref, rw_ref, sel_ref, qw_ref,
    d_out, v_out, mn_out, md_out, di_out, ce_out, ai_out, as_out,
):
    f = lambda a: float(np.float32(a))
    outs = {"mn": mn_out, "md": md_out, "di": di_out, "ai": ai_out, "as": as_out}

    def plane(z):
        for j in range(4):
            own = pl.ds(j, 32, stride=4)
            xe, xw = re_ref[z, own, :], rw_ref[z, own, :]
            vs = [v_ref[c, z, own, :] for c in range(3)] + [expand(xe, xw, 3, 1)]
            ds = [d_ref[c, z, own, :] for c in range(3)] + [expand(xe, xw, 0, 1)]
            for ch in range(4):
                v_out[ch, z, j] = vs[ch]
                d_out[ch, z, j] = ds[ch] + DT * vs[ch]
            mods = [m_ref[z, own, :], expand(xe, xw, 6, 0)]
            rhos = [r_ref[z, own, :], strip_density(expand(xe, xw, 7, 0))]
            for m in range(2):

                def put(name, x):
                    at = (m, j) if name in ("ai", "as") else (m, z, j)
                    outs[name][at] = x

                fields(mods[m], rhos[m], j, z, put)
            weight = qw_ref[...] * (f(W[z]) * f(PERIODIC[j]))
            ce_out[z, j] = east_coefs(mods[0], mods[1], sel_ref[...], weight)

    for z in range(5):
        plane(z)


OWN_SHAPES = ((4, 5, 4, 32, N),) * 2 + ((2, 5, 4, 32, N),) * 3 + ((5, 4, 32, 256),) + ((2, 4, 32, N),) * 2


def early(d, v, m, r, re, rw, sel, qw):
    whole = pl.BlockSpec(memory_space=pltpu.VMEM)
    return pl.pallas_call(
        early_kernel,
        in_specs=[whole] * 8,
        out_specs=[whole] * 8,
        out_shape=[jax.ShapeDtypeStruct(x, F32) for x in OWN_SHAPES],
        compiler_params=pltpu.CompilerParams(vmem_limit_bytes=16 * 1024 * 1024),
        name="early",
    )(d, v, m, r, re, rw, sel, qw)


def prepare_kernel(*refs):
    halos, tables, refs = refs[14:18], refs[18:22], refs[22:]
    (d0, d1, d2, d3, v0, v1, v2, v3), refs = refs[:8], refs[8:]
    (mn_ref, md_ref, di_ref, ce_ref, ai_ref, as_ref), refs = refs[:6], refs[6:]
    (k0, k1, k2, k3, n0, n1, n2, n3), refs = refs[:8], refs[8:]
    buffers, (halo_sem,) = refs[:8], refs[8:]
    d_ref, v_ref = (d0, d1, d2, d3), (v0, v1, v2, v3)
    copy = pltpu.make_async_copy
    late = [copy(x, y, halo_sem.at[i]) for i, (x, y) in enumerate(zip((*halos, *tables), buffers))]
    for c in late:
        c.start()
    n_ref, s_ref, cn_ref, cs_ref, sel_ref, qw_ref, grad_ref, back_ref = buffers
    outs = {"mn": mn_ref, "md": md_ref, "di": di_ref, "ai": ai_ref, "as": as_ref}
    f = lambda a: float(np.float32(a))
    for c in late:
        c.wait()

    def halo(at, j, north=n_ref, south=s_ref):
        at = (*at, pl.ds(j, 4, stride=4), slice(None))
        return jnp.concatenate([north[at], south[at]], axis=0)

    rest = slice(32, E)
    mains, sides = [], []
    for z in range(5):
        for j in range(4):
            xe, xw, mod, rho = (halo((i, z), j, cn_ref, cs_ref) for i in (2, 3, 0, 1))
            vs = [halo((3 + c, z), j) for c in range(3)] + [expand(xe, xw, 3, 1)]
            ds = [halo((c, z), j) for c in range(3)] + [expand(xe, xw, 0, 1)]
            for ch in range(4):
                v_ref[ch][z, j, rest] = vs[ch]
                d_ref[ch][z, j, rest] = ds[ch] + DT * vs[ch]
            mods = [mod, expand(xe, xw, 6, 0)]
            rhos = [rho, strip_density(expand(xe, xw, 7, 0))]
            for m in range(2):

                def put(name, x):
                    at = (m, j, rest) if name in ("ai", "as") else (m, z, j, rest)
                    outs[name][at] = x

                fields(mods[m], rhos[m], j, z, put)
            mains.append(mods[0])
            sides.append(mods[1])
    c = east_coefs(jnp.concatenate(mains), jnp.concatenate(sides), sel_ref[...], qw_ref[...])
    for z in range(5):
        for j in range(4):
            at = (z * 4 + j) * 8
            ce_ref[z, j, rest] = c[at : at + 8] * (f(W[z]) * f(PERIODIC[j]))
    for m in range(2):
        for z in range(5):
            mn_ref[m, z, 4] = pltpu.roll(mn_ref[m, z, 0], E - 1, 0)

    def emit(ch, j, z, d, k):
        m = ch // 3
        v = v_ref[ch][z, j]
        if z == 0:
            k = k + ai_ref[m, j] * v + as_ref[m, j] * d
        v_ref[ch][z, j] = v - di_ref[m, z, j] * k

    line_forces(
        d_ref, (k0, k1, k2, k3), (n0, n1, n2, n3), mn_ref, md_ref, ce_ref, grad_ref, back_ref, 4, emit
    )


def prepare(fetched, halos, tables):
    grad, back, sel, qw = tables
    whole = pl.BlockSpec(memory_space=pltpu.VMEM)
    late = (*halos, sel, qw, grad, back)
    return pl.pallas_call(
        prepare_kernel,
        in_specs=[whole] * 14 + [pl.BlockSpec(memory_space=pltpu.HBM)] * 8,
        out_specs=[whole] * 14,
        out_shape=PREPARED,
        input_output_aliases={i: i for i in range(14)},
        scratch_shapes=[pltpu.VMEM((5, 4, E, N), F32)] * 8
        + [pltpu.VMEM(x.shape, x.dtype) for x in late]
        + [pltpu.SemaphoreType.DMA((8,))],
        compiler_params=pltpu.CompilerParams(vmem_limit_bytes=VMEM_LIMIT),
        name="prepare",
    )(*fetched, *in_hbm(*late))


def steps_kernel(
    i0, i1, i2, i3, u0, u1, u2, u3, mn_ref, md_ref, di_ref, ce_ref, ai_ref, as_ref,
    b_ref, bs_ref, bn_ref, bo_ref, grad_ref, back_ref,
    dout_ref, vout_ref,
    d0, d1, d2, d3, v0, v1, v2, v3, k0, k1, k2, k3, n0, n1, n2, n3, f_ref,
):
    d_in, v_in = (i0, i1, i2, i3), (u0, u1, u2, u3)
    d_ref, v_ref = (d0, d1, d2, d3), (v0, v1, v2, v3)
    k_ref, kn_ref = (k0, k1, k2, k3), (n0, n1, n2, n3)
    for t in range(3):
        n, at = FORCE_ROWS[t]
        gap = jnp.zeros((8 - n // 2, N), F32)
        for ch in range(4):
            for j in range(4):
                own = pl.ds(j, 32, stride=4)
                x = b_ref[t, ch, own, :] if ch < 3 else bs_ref[t, own, :]
                halo = pl.ds(at + j, n // 4, stride=4)
                f_ref[t, ch, j] = jnp.concatenate(
                    [x, bn_ref[ch, halo, :], gap, bo_ref[ch, halo, :]], axis=0
                )
    for ch in range(3):
        for j in range(4):
            x = b_ref[3, ch, pl.ds(j, 32, stride=4), :]
            f_ref[3, ch, j] = jnp.concatenate([x, jnp.zeros((8, N), F32)], axis=0)

    for ch in range(4):
        for j in range(4):
            for z in range(5):
                v = v_in[ch][z, j]
                if z == 0:
                    v = v + di_ref[ch // 3, z, j] * f_ref[0, ch, j]
                v_ref[ch][z, j] = v
                d_ref[ch][z, j] = d_in[ch][z, j] + DT * v

    def velocity(t, ch, j, z, d, k):
        m = ch // 3
        n = slice(0, d.shape[0])
        v = v_ref[ch][z, j, n]
        if z == 0:
            k = k + ai_ref[m, j, n] * v + as_ref[m, j, n] * d - f_ref[t, ch, j, n]
        return v - di_ref[m, z, j, n] * k

    def step(t, carry):
        def emit(ch, j, z, d, k):
            v = velocity(t, ch, j, z, d, k)
            v_ref[ch][z, j] = v
            d_ref[ch][z, j] = d + DT * v

        line_forces(d_ref, k_ref, kn_ref, mn_ref, md_ref, ce_ref, grad_ref, back_ref, 4, emit)
        return carry

    lax.fori_loop(1, 3, step, 0)

    def final(ch, j, z, d, k):
        dout_ref[ch, z, pl.ds(j, 32, stride=4), :] = d
        vout_ref[ch, z, pl.ds(j, 32, stride=4), :] = velocity(3, ch, j, z, d, k)

    line_forces(d_ref, k_ref, kn_ref, mn_ref, md_ref, ce_ref, grad_ref, back_ref, 3, final)


def steps(prepared, b, bs, bn, bo, tables):
    grad, back = tables[:2]
    whole = pl.BlockSpec(memory_space=pltpu.VMEM)
    return pl.pallas_call(
        steps_kernel,
        in_specs=[whole] * 20,
        out_specs=[whole] * 2,
        out_shape=[jax.ShapeDtypeStruct((3, 5, N, N), F32)] * 2,
        scratch_shapes=[pltpu.VMEM((5, 4, E, N), F32)] * 16 + [pltpu.VMEM((4, 4, 4, E, N), F32)],
        compiler_params=pltpu.CompilerParams(vmem_limit_bytes=VMEM_LIMIT),
        name="steps",
    )(*prepared, b, bs, bn, bo, grad, back)


def local(displacement, velocity, modulus, density, traces, record_row):
    tables = tuple(jnp.asarray(t) for t in east_tables())
    west, east, north, south, late_north, late_south, sent = begin(
        displacement, velocity, modulus, density, jnp.transpose(traces[0], (1, 0, 2)), record_row
    )
    from_east = shifted(west, "reg", -1)
    from_west = shifted(east, "reg", 1)
    from_north = shifted(south, "src", -1)
    from_south = shifted(north, "src", 1)
    arrived = lax.all_to_all(
        sent.reshape(N, 40, N), ("src", "reg"), split_axis=0, concat_axis=0, tiled=True
    )
    corner = jnp.stack([from_east, from_west])
    late_south = jnp.concatenate([late_south, corner[:, :, :H]], axis=0)
    late_north = jnp.concatenate([late_north, corner[:, :, N - H :]], axis=0)
    corner_north = shifted(late_south, "src", -1)
    corner_south = shifted(late_north, "src", 1)
    co = coefs(modulus, density, from_east, from_west)
    own = early(displacement, velocity, modulus, density, from_east, from_west, *tables[2:])
    b, b_strip, b_north, b_south, *fetched = place(arrived, co, own)
    b_from_south = shifted(b_north, "src", 1)
    b_from_north = shifted(b_south, "src", -1)
    from_north, from_south, corner_north, corner_south, _ = lax.optimization_barrier(
        (from_north, from_south, corner_north, corner_south, b)
    )
    prepared = prepare(fetched, (from_north, from_south, corner_north, corner_south), tables)
    return steps(prepared, b, b_strip, b_from_north, b_from_south, tables)


def solution(mesh):
    state = P(None, None, "src", "reg")
    field = P(None, "src", "reg")
    in_specs = (state, state, field, field, P(("src", "reg"), None, None, None), P(("src", "reg"), None))
    return jax.shard_map(local, mesh=mesh, in_specs=in_specs, out_specs=(state, state), check_vma=False)
```

```python
import math

import jax
import jax.numpy as jnp
import numpy as np
from jax import lax
from jax.experimental import pallas as pl
from jax.experimental.pallas import tpu as pltpu
from jax.sharding import PartitionSpec as P


F32 = jnp.float32
BF16 = jnp.bfloat16
STEPS = 4
DT = 0.02
N = 128
H = 16
E = 40
FORCE_ROWS = ((12, 0), (8, 12), (4, 20))
VMEM_LIMIT = 28 * 1024 * 1024


def gll():
    inner = math.sqrt(3.0 / 7.0)
    x = np.array([-1.0, -inner, 0.0, inner, 1.0])
    w = np.array([0.1, 49.0 / 90.0, 32.0 / 45.0, 49.0 / 90.0, 0.1])
    leg = (35.0 * x**4 - 30.0 * x**2 + 3.0) / 8.0
    d = np.zeros((5, 5))
    for i in range(5):
        for j in range(5):
            if i != j:
                d[i, j] = leg[i] / (leg[j] * (x[i] - x[j]))
    d[0, 0] = -5.0
    d[4, 4] = 5.0
    return d, w


DER, W = gll()
PERIODIC = [2 * W[0], W[1], W[2], W[3]]


def network():
    odd = [[(DER[i, 0] - DER[i, 4]) / 2, (DER[i, 1] - DER[i, 3]) / 2] for i in (0, 1)]
    even = [[(DER[i, 0] + DER[i, 4]) / 2, (DER[i, 1] + DER[i, 3]) / 2] for i in (0, 1)]
    scale = [even[0][0], even[1][0], DER[2, 0]]
    f = lambda x: float(np.float32(x))
    p = [[f(odd[i][k] / scale[i]) for k in range(2)] for i in range(2)]
    q = [f(even[i][1] / scale[i]) for i in range(2)]
    scale = np.array(scale + scale[1::-1])
    return p, q, f(DER[2, 1] / DER[2, 0]), W * scale**2


ODD, EVEN, MIDDLE, POINT = network()


def slopes(v):
    twice = v[2] + v[2]
    u0, u1 = (v[0] + v[4]) - twice, (v[1] + v[3]) - twice
    m0, m1 = v[0] - v[4], v[1] - v[3]
    out = [None] * 5
    for i in (0, 1):
        p = ODD[i][0] * m0 + ODD[i][1] * m1
        q = u0 + EVEN[i] * u1
        out[i], out[4 - i] = p + q, p - q
    out[2] = m0 + MIDDLE * m1
    return out


def tested(f):
    ep, eq = [f[0] + f[4], f[1] + f[3]], [f[0] - f[4], f[1] - f[3]]
    m0 = (ODD[0][0] * ep[0] + ODD[1][0] * ep[1]) + f[2]
    m1 = (ODD[0][1] * ep[0] + ODD[1][1] * ep[1]) + MIDDLE * f[2]
    u0 = eq[0] + eq[1]
    u1 = EVEN[0] * eq[0] + EVEN[1] * eq[1]
    return [u0 + m0, u1 + m1, -2.0 * (u0 + u1), u1 - m1, u0 - m0]


def column_of(x, comp):
    if 0 <= x < N:
        return x
    return N + 32 * comp + (x - N if x >= N else x + 32)


def east_tables():
    grad = np.zeros((3, 256, 256))
    sel = np.zeros((256, 256))
    weight = np.zeros((1, 256))
    for k in range(E):
        for i in range(5):
            q = i * E + k
            xi = 4 * (k - 4) + i
            weight[0, q] = 0.5 * W[i]
            if xi < N + H:
                sel[column_of(xi, 0), q] = 1.0
            for comp in range(3):
                for j in range(5):
                    xj = 4 * (k - 4) + j
                    if xj < N + H:
                        grad[comp, column_of(xj, comp), q] = DER[i, j]

    def two(a):
        hi = a.astype(np.float32).astype(jnp.bfloat16)
        lo = (a - hi.astype(np.float64)).astype(np.float32).astype(jnp.bfloat16)
        return np.stack([hi, lo], axis=1)

    back = np.ascontiguousarray(np.swapaxes(grad, 1, 2))
    return two(grad), two(back), sel.astype(jnp.bfloat16), weight.astype(np.float32)


def shifted(block, axis, distance):
    n = lax.axis_size(axis)
    return lax.ppermute(block, axis, [((i - distance) % n, i) for i in range(n)])


def in_hbm(*arrays):
    return [pltpu.with_memory_space_constraint(x, pltpu.HBM) for x in arrays]


def dot(a, b):
    return jnp.dot(a, b, preferred_element_type=F32)


def split2(x):
    hi = x.astype(BF16)
    return hi, (x - hi.astype(F32)).astype(BF16)


def lane_ids(shape):
    return lax.broadcasted_iota(jnp.int32, shape, len(shape) - 1)


def east_weight(shape):
    r = lane_ids(shape) % 4
    f = lambda a: float(np.float32(a))
    return jnp.where(r == 0, f(PERIODIC[0]), jnp.where(r == 2, f(PERIODIC[2]), f(PERIODIC[1])))


def moved(x, shift):
    return pltpu.roll(x, shift % N, x.ndim - 1) if shift % N else x


def lane_move(x, shift, start, width=16):
    shift %= 128
    y = pltpu.roll(x, shift, x.ndim - 1) if shift else x
    lane = lane_ids(x.shape)
    return jnp.where((lane >= start) & (lane < start + width), y, 0.0)


WEST_GROUPS = ((0, 12, 116, 0), (21, 8, 120, 1), (34, 4, 124, 2))
EAST_GROUPS = ((12, 9, 0, 0), (29, 5, 0, 1), (38, 1, 0, 2))
TO_WEST = (0, 32, 64, 96, 16, 48, 80, 112)
TO_EAST = (112, 16, 48, 80, 0, 32, 64, 96)


def begin_kernel(
    d_ref, v_ref, m_ref, r_ref, tr_ref, id_ref,
    west_ref, east_ref, north_ref, south_ref, ln_ref, ls_ref, sent_ref,
    buf, west_buf, east_buf, tr_buf, sent_buf, id_buf, row_buf, in_sem, row_sem, out_sem, tr_sem, sent_sem,
):
    copy = pltpu.make_async_copy
    face_rows = copy(id_ref, row_buf, sent_sem.at[8])
    face_rows.start()
    loads = []
    for z in range(5):
        loads.append(
            [
                copy(d_ref.at[:, z], buf.at[z, 0:3], in_sem.at[z, 0]),
                copy(v_ref.at[:, z], buf.at[z, 3:6], in_sem.at[z, 1]),
                copy(m_ref.at[z], buf.at[z, 6], in_sem.at[z, 2]),
                copy(r_ref.at[z], buf.at[z, 7], in_sem.at[z, 3]),
            ]
        )
        for c in loads[z]:
            c.start()
    records = []
    for g in range(8):
        at = pl.ds(64 * g, 64)
        records.append(copy(tr_ref.at[:, at], tr_buf.at[:, at], tr_sem.at[g]))
        records[g].start()
    lane = lane_ids((N, N))
    stores = []
    for z in range(5):
        for c in loads[z]:
            c.wait()
        for i, (at, top, low) in enumerate(
            ((slice(0, 6), north_ref, south_ref), (slice(6, 8), ln_ref, ls_ref))
        ):
            stores.append(copy(buf.at[z, at, N - H : N], top.at[:, z], row_sem.at[z, 2 * i]))
            stores.append(copy(buf.at[z, at, 0:H], low.at[:, z], row_sem.at[z, 2 * i + 1]))
        for c in stores[-4:]:
            c.start()
        packed = []
        for h in range(2):
            x = buf[z, 4 * h]
            for a in range(1, 4):
                mask = (lane >= 32 * a - 16) & (lane < 32 * a + 16)
                x = jnp.where(mask, pltpu.roll(buf[z, 4 * h + a], 32 * a, 1), x)
            packed.append(x)
        other = pltpu.roll(packed[1], 16, 1)
        west_buf[z] = jnp.where(lane % 32 < 16, packed[0], other)
        east_buf[z] = jnp.where(lane % 32 < 16, other, packed[0])
        stores.append(copy(west_buf.at[z], west_ref.at[z], out_sem.at[z, 0]))
        stores.append(copy(east_buf.at[z], east_ref.at[z], out_sem.at[z, 1]))
        for c in stores[-2:]:
            c.start()
    face_rows.wait()
    mine = lane_ids((N, 4 * N)) // STEPS == lax.broadcasted_iota(jnp.int32, (N, 4 * N), 0)
    spread = jnp.where(mine, jnp.broadcast_to(row_buf[...].astype(F32), (N, 4 * N)), 0.0).astype(BF16)
    step = lax.broadcasted_iota(jnp.int32, (4 * N, N), 0) % STEPS == lane_ids((4 * N, N))
    id_buf[...] = dot(spread, jnp.where(step, 1.0, 0.0).astype(BF16))
    lane = lane_ids((16, N))
    for g in range(8):
        records[g].wait()
        first = 640 * g
        for d in range(16):
            for k in range(9):
                sent_buf[pl.ds(first + 40 * d + 4 * k, 4), :] = tr_buf[k, pl.ds(64 * g + 4 * d, 4), :]
        ids = id_buf[16 * g : 16 * g + 16, :]
        ids = (
            ids
            + pltpu.roll(pltpu.roll(ids, 1, 0), 4, 1)
            + pltpu.roll(pltpu.roll(ids, 15, 0), 8, 1)
        )
        extra = [ids]
        for rho in range(3):
            sides = [jnp.zeros((16, N), F32)] * 2
            for c in range(3):
                for t in range(3):
                    x = tr_buf[3 * rho + c, pl.ds(64 * g + t, 16, stride=4), :]
                    for i, groups in enumerate((WEST_GROUPS, EAST_GROUPS)):
                        off, width, col, _ = groups[t]
                        at = 40 * c + off
                        y = pltpu.roll(x, (at - col) % N, 1) if (at - col) % N else x
                        sides[i] = jnp.where((lane >= at) & (lane < at + width), y, sides[i])
            extra.append(pltpu.roll(sides[0], 1, 0) + pltpu.roll(sides[1], 15, 0))
        for i, x in enumerate(extra):
            for h in range(2):
                sent_buf[pl.ds(first + 320 * h + 36 + i, 8, stride=40), :] = x[8 * h : 8 * h + 8]
        at = pl.ds(first, 640)
        stores.append(copy(sent_buf.at[at], sent_ref.at[at], sent_sem.at[g]))
        stores[-1].start()
    for c in stores:
        c.wait()


def begin(d, v, m, r, records, ids):
    hbm = pl.BlockSpec(memory_space=pltpu.HBM)
    dma = pltpu.SemaphoreType.DMA
    return pl.pallas_call(
        begin_kernel,
        in_specs=[hbm] * 6,
        out_specs=[hbm] * 7,
        out_shape=[pltpu.HBM((5, N, N), F32)] * 2
        + [pltpu.HBM((6, 5, H, N), F32)] * 2
        + [pltpu.HBM((2, 5, H, N), F32)] * 2
        + [pltpu.HBM((40 * N, N), F32)],
        scratch_shapes=[
            pltpu.VMEM((5, 8, N, N), F32),
            pltpu.VMEM((5, N, N), F32),
            pltpu.VMEM((5, N, N), F32),
            pltpu.VMEM((9, 4 * N, N), F32),
            pltpu.VMEM((40 * N, N), F32),
            pltpu.VMEM((N, N), F32),
            pltpu.VMEM((1, STEPS * N), jnp.int32),
            dma((5, 4)),
            dma((5, 4)),
            dma((5, 2)),
            dma((8,)),
            dma((9,)),
        ],
        compiler_params=pltpu.CompilerParams(vmem_limit_bytes=20 * 1024 * 1024),
        name="begin",
    )(*in_hbm(d, v, m, r, records, ids))


def coefs_kernel(m_ref, r_ref, re_ref, rw_ref, out_ref):
    f = lambda a: float(np.float32(a))
    shape = (N, N)
    lane = lane_ids(shape)
    row = lax.broadcasted_iota(jnp.int32, shape, 0) % 4
    pick = lambda n: jnp.where(
        n == 0, f(PERIODIC[0]), jnp.where(n == 2, f(PERIODIC[2]), f(PERIODIC[1]))
    )

    def three(at, mod, rho, ew):
        area = 0.25 * ew * pick(row)
        out_ref[at] = area
        out_ref[at + 1] = area * jnp.sqrt(rho * mod)
        out_ref[at + 2] = area * (0.5 * mod)

    three(0, m_ref[0], r_ref[0], pick(lane % 4))
    mod = rho = jnp.ones(shape, F32)
    node = jnp.zeros(shape, jnp.int32)
    for groups, src, base, at_lane in (
        (WEST_GROUPS, rw_ref[0], 112, TO_EAST),
        (EAST_GROUPS, re_ref[0], 0, TO_WEST),
    ):
        for c in range(3):
            for off, width, col, _ in groups:
                at = 40 * c + off
                mask = (lane >= at) & (lane < at + width)
                mod = jnp.where(mask, moved(src, at - at_lane[6] - (col - base)), mod)
                rho = jnp.where(mask, moved(src, at - at_lane[7] - (col - base)), rho)
                node = jnp.where(mask, lane - at, node)
    three(3, mod, rho, pick(node % 4))


def coefs(m, r, re, rw):
    plane = pl.BlockSpec((1, N, N), lambda i: (0, 0, 0))
    return pl.pallas_call(
        coefs_kernel,
        grid=(1,),
        in_specs=[plane] * 4,
        out_specs=pl.BlockSpec((6, N, N), lambda i: (0, 0, 0)),
        out_shape=jax.ShapeDtypeStruct((6, N, N), F32),
        name="coefs",
    )(m, r, re, rw)


def place_kernel(*refs):
    (arr_ref, co_hbm), own, refs = refs[:2], refs[2:11], refs[11:]
    (b_ref, strip_ref, north_ref, south_ref), fetched, refs = refs[:4], refs[4:22], refs[22:]
    inj_ref, side_ref, vid_ref, ids_ref, co_ref, sem, own_sem = refs
    copy = pltpu.make_async_copy
    lane = lane_ids((N, N))
    plane = jnp.where(lane < 8, lane % 4, lane - 5)
    slot = jnp.where(lane < 4, 16, 8)
    where_to = (arr_ref[:, 36, :].astype(jnp.int32) + N * plane) * slot
    vid_ref[...] = jnp.transpose(where_to)[:16]
    to_scalar = copy(vid_ref, ids_ref, sem.at[0])
    to_scalar.start()
    to_co = copy(co_hbm, co_ref, sem.at[1])
    to_co.start()
    node = pl.ds(0, 32)
    moves = []
    for ch in range(4):
        moves.append((own[0].at[ch], fetched[ch].at[:, :, node]))
        moves.append((own[1].at[ch], fetched[4 + ch].at[:, :, node]))
    for m in range(2):
        moves.append((own[2].at[m], fetched[8].at[m, :, 0:4, node]))
        moves.append((own[3].at[m], fetched[9].at[m, :, :, node]))
        moves.append((own[4].at[m], fetched[10].at[m, :, :, node]))
    for i in (5, 6, 7):
        moves.append((own[i], fetched[6 + i].at[:, :, node]))
    moves.extend((own[8].at[ch], fetched[14 + ch]) for ch in range(4))
    moves = [copy(x, y, own_sem.at[i]) for i, (x, y) in enumerate(moves)]
    to_scalar.wait()
    for c in moves:
        c.start()

    def body(s, carry):
        tail = arr_ref[s, 32:40, :]
        for t in range(STEPS):
            at = pl.multiple_of(ids_ref[t, s], 16)
            inj_ref[pl.ds(at, 8), :] = arr_ref[s, pl.ds(t, 8, stride=4), :]
            inj_ref[pl.ds(at + 8, 8), :] = tail
        for i in range(2):
            for t in range(3):
                side_ref[pl.ds(pl.multiple_of(ids_ref[4 + 4 * i + t, s], 8), 8), :] = tail
        return carry

    lax.fori_loop(0, 128, body, 0, unroll=8)
    to_co.wait()
    lane = lane_ids((8, N))

    def combine(k, carry):
        y = pl.multiple_of(k * 8, 8)
        rows = pl.ds(y, 8)
        co = [co_ref[i, rows, :] for i in range(6)]
        for t in range(STEPS):
            for c in range(3):
                base = (t * N + y) * 16
                inc = inj_ref[pl.ds(base + c, 8, stride=16), :]
                vel = inj_ref[pl.ds(base + 3 + c, 8, stride=16), :]
                dis = inj_ref[pl.ds(base + (6 + c if c < 2 else 8 + t), 8, stride=16), :]
                b_ref[t, c, rows, :] = co[0] * inc + co[1] * vel + co[2] * dis
        b = None
        for rho in range(3):
            x = jnp.zeros((8, N), F32)
            for i, groups in enumerate((WEST_GROUPS, EAST_GROUPS)):
                for off, width, _, t in groups:
                    part = side_ref[pl.ds(((3 * i + t) * N + y) * 8 + 5 + rho, 8, stride=8), :]
                    mask = (lane >= off) & (lane < off + width)
                    for c in (1, 2):
                        mask = mask | ((lane >= 40 * c + off) & (lane < 40 * c + off + width))
                    x = jnp.where(mask, part, x)
            b = co[3] * x if b is None else b + co[3 + rho] * x
        for t in range(3):
            out = None
            for c in range(3):
                off, width, col, _ = WEST_GROUPS[t]
                start = 32 * c + 16 + col - 112
                p = lane_move(b, start - 40 * c - off, start, width)
                off, width, _, _ = EAST_GROUPS[t]
                p = p + lane_move(b, 32 * c - 40 * c - off, 32 * c, width)
                out = p if out is None else out + p
            strip_ref[t, rows, :] = out
        return carry

    lax.fori_loop(0, 16, combine, 0)
    for t in range(3):
        n, at = FORCE_ROWS[t]
        for ch in range(4):
            x = b_ref.at[t, ch] if ch < 3 else strip_ref.at[t]
            north_ref[ch, at : at + n] = x[N - n :, :]
            south_ref[ch, at : at + n] = x[:n, :]
    for c in moves:
        c.wait()


PREPARED = (
    *[jax.ShapeDtypeStruct((5, 4, E, N), F32)] * 8,
    jax.ShapeDtypeStruct((2, 5, 5, E, N), F32),
    jax.ShapeDtypeStruct((2, 5, 4, E, N), F32),
    jax.ShapeDtypeStruct((2, 5, 4, E, N), F32),
    jax.ShapeDtypeStruct((5, 4, E, 256), F32),
    jax.ShapeDtypeStruct((2, 4, E, N), F32),
    jax.ShapeDtypeStruct((2, 4, E, N), F32),
)


def place(arrived, co, own):
    whole = pl.BlockSpec(memory_space=pltpu.VMEM)
    return pl.pallas_call(
        place_kernel,
        in_specs=[whole] + [pl.BlockSpec(memory_space=pltpu.HBM)] * 10,
        out_specs=[whole] * 22,
        out_shape=[
            jax.ShapeDtypeStruct((STEPS, 3, N, N), F32),
            jax.ShapeDtypeStruct((3, N, N), F32),
            jax.ShapeDtypeStruct((4, 24, N), F32),
            jax.ShapeDtypeStruct((4, 24, N), F32),
            *PREPARED,
            *[jax.ShapeDtypeStruct((5, 4, 32, N), F32)] * 4,
        ],
        scratch_shapes=[
            pltpu.VMEM((STEPS * N * 16, N), F32),
            pltpu.VMEM((6 * N * 8, N), F32),
            pltpu.VMEM((16, N), jnp.int32),
            pltpu.SMEM((16, N), jnp.int32),
            pltpu.VMEM((6, N, N), F32),
            pltpu.SemaphoreType.DMA((2,)),
            pltpu.SemaphoreType.DMA((21,)),
        ],
        compiler_params=pltpu.CompilerParams(vmem_limit_bytes=VMEM_LIMIT),
        name="place",
    )(arrived, *in_hbm(co, *own))


def line_forces(d, k, kn, mn_ref, md_ref, ce_ref, grad_ref, back_ref, channels, emit):
    live = E if channels == 4 else 32
    rows = 5 * 4 * live

    def north(ch):
        m = ch // 3
        for z in range(5):
            v = [d[ch][z, j] for j in range(4)]
            v.append(pltpu.roll(v[0], E - 1, 0))
            g = slopes(v)
            r = tested([g[i] * mn_ref[m, z, i] for i in range(5)])
            r[0] = r[0] + pltpu.roll(r[4], 1, 0)
            for j in range(4):
                kn[ch][z, j] = r[j]

    def depth(ch):
        m = ch // 3
        for j in range(4):
            x = [d[ch][z, j, :live] for z in range(5)]
            g = slopes(x)
            r = tested([g[z] * md_ref[m, z, j, :live] for z in range(5)])
            for z in range(5):
                emit(ch, j, z, x[z], (k[ch][z, j, :live] + kn[ch][z, j, :live]) + r[z])

    sh, sl = split2(d[3][:, :, :live].reshape(rows, N))
    strip = None
    for c in range(3):
        mh, ml = split2(d[c][:, :, :live].reshape(rows, N))
        hi = jnp.concatenate([mh, sh], axis=1)
        lo = jnp.concatenate([ml, sl], axis=1)
        g = dot(hi, grad_ref[c, 0]) + dot(lo, grad_ref[c, 0]) + dot(hi, grad_ref[c, 1])
        fh, fl = split2(g * ce_ref[:, :, :live].reshape(rows, 256))
        f = dot(fh, back_ref[c, 0]) + dot(fl, back_ref[c, 0]) + dot(fh, back_ref[c, 1])
        k[c][:, :, :live] = f[:, :N].reshape(5, 4, live, N)
        if channels == 4:
            strip = f[:, N:] if strip is None else strip + f[:, N:]
        north(c)
        if c:
            depth(c - 1)
    if channels == 4:
        north(3)
        k[3][...] = strip.reshape(5, 4, E, N)
    depth(2)
    if channels == 4:
        depth(3)


def row_forces(d, k, at, into, n, md_ref, ce_ref, grad_ref, back_ref):
    rows = 5 * 4 * n
    sh, sl = split2(d[3][:, :, at].reshape(rows, N))
    strip = None
    for c in range(3):
        mh, ml = split2(d[c][:, :, at].reshape(rows, N))
        hi = jnp.concatenate([mh, sh], axis=1)
        lo = jnp.concatenate([ml, sl], axis=1)
        g = dot(hi, grad_ref[c, 0]) + dot(lo, grad_ref[c, 0]) + dot(hi, grad_ref[c, 1])
        fh, fl = split2(g * ce_ref[:, :, at].reshape(rows, 256))
        f = dot(fh, back_ref[c, 0]) + dot(fl, back_ref[c, 0]) + dot(fh, back_ref[c, 1])
        k[c][:, :, into] = f[:, :N].reshape(5, 4, n, N)
        strip = f[:, N:] if strip is None else strip + f[:, N:]
    k[3][:, :, into] = strip.reshape(5, 4, n, N)
    for ch in range(4):
        for j in range(4):
            g = slopes([d[ch][z, j, at] for z in range(5)])
            r = tested([g[z] * md_ref[ch // 3, z, j, at] for z in range(5)])
            for z in range(5):
                k[ch][z, j, into] = k[ch][z, j, into] + r[z]


def expand(xe, xw, first, step):
    out = None
    for c in range(3):
        p = lane_move(xe, 32 * c - TO_WEST[first + step * c], 32 * c)
        p = p + lane_move(xw, 32 * c + 16 - TO_EAST[first + step * c], 32 * c + 16)
        out = p if out is None else out + p
    return out


def fields(mod, rho, j, z, put):
    f = lambda a: float(np.float32(a))
    ew = east_weight(mod.shape)
    half = 0.5 * mod * ew
    put("mn", half * f(POINT[j] * W[z]))
    put("md", half * f(POINT[z] * PERIODIC[j]))
    put("di", DT / (0.125 * rho * ew * (f(PERIODIC[j]) * f(W[z]))))
    if z == 0:
        area = 0.25 * ew * f(PERIODIC[j])
        put("ai", area * jnp.sqrt(rho * mod))
        put("as", area * (0.5 * mod))


def east_coefs(main, strip, sel, weight):
    x = jnp.concatenate([main, strip], axis=1)
    hi = x.astype(BF16)
    mid, lo = split2(x - hi.astype(F32))
    return (dot(hi, sel) + dot(mid, sel) + dot(lo, sel)) * weight


def strip_density(rho):
    return jnp.where(lane_ids(rho.shape) < 96, rho, 1.0)


def early_kernel(
    d_ref, v_ref, m_ref, r_ref, re_ref, rw_ref, sel_ref, qw_ref, grad_ref, back_ref,
    d_out, v_out, mn_out, md_out, di_out, ce_out, ai_out, as_out, k_out,
):
    f = lambda a: float(np.float32(a))
    outs = {"mn": mn_out, "md": md_out, "di": di_out, "ai": ai_out, "as": as_out}

    def plane(z):
        for j in range(4):
            own = pl.ds(j, 32, stride=4)
            xe, xw = re_ref[z, own, :], rw_ref[z, own, :]
            vs = [v_ref[c, z, own, :] for c in range(3)] + [expand(xe, xw, 3, 1)]
            ds = [d_ref[c, z, own, :] for c in range(3)] + [expand(xe, xw, 0, 1)]
            for ch in range(4):
                v_out[ch, z, j] = vs[ch]
                d_out[ch, z, j] = ds[ch] + DT * vs[ch]
            mods = [m_ref[z, own, :], expand(xe, xw, 6, 0)]
            rhos = [r_ref[z, own, :], strip_density(expand(xe, xw, 7, 0))]
            for m in range(2):

                def put(name, x):
                    at = (m, j) if name in ("ai", "as") else (m, z, j)
                    outs[name][at] = x

                fields(mods[m], rhos[m], j, z, put)
            weight = qw_ref[...] * (f(W[z]) * f(PERIODIC[j]))
            ce_out[z, j] = east_coefs(mods[0], mods[1], sel_ref[...], weight)

    for z in range(5):
        plane(z)
    node = slice(0, 32)
    d, k = [d_out.at[ch] for ch in range(4)], [k_out.at[ch] for ch in range(4)]
    row_forces(d, k, node, node, 32, md_out, ce_out, grad_ref, back_ref)


OWN_SHAPES = (
    *((4, 5, 4, 32, N),) * 2,
    *((2, 5, 4, 32, N),) * 3,
    (5, 4, 32, 256),
    *((2, 4, 32, N),) * 2,
    (4, 5, 4, 32, N),
)


def early(d, v, m, r, re, rw, tables):
    grad, back, sel, qw = tables
    whole = pl.BlockSpec(memory_space=pltpu.VMEM)
    return pl.pallas_call(
        early_kernel,
        in_specs=[whole] * 10,
        out_specs=[whole] * 9,
        out_shape=[jax.ShapeDtypeStruct(x, F32) for x in OWN_SHAPES],
        compiler_params=pltpu.CompilerParams(vmem_limit_bytes=16 * 1024 * 1024),
        name="early",
    )(d, v, m, r, re, rw, sel, qw, grad, back)


def prepare_kernel(*refs):
    own_k, halos, tables, refs = refs[14:18], refs[18:22], refs[22:26], refs[26:]
    (d0, d1, d2, d3, v0, v1, v2, v3), refs = refs[:8], refs[8:]
    (mn_ref, md_ref, di_ref, ce_ref, ai_ref, as_ref), refs = refs[:6], refs[6:]
    halo_k, refs = refs[:4], refs[4:]
    buffers, (halo_sem,) = refs[:8], refs[8:]
    d_ref, v_ref = (d0, d1, d2, d3), (v0, v1, v2, v3)
    copy = pltpu.make_async_copy
    late = [copy(x, y, halo_sem.at[i]) for i, (x, y) in enumerate(zip((*halos, *tables), buffers))]
    for c in late:
        c.start()
    n_ref, s_ref, cn_ref, cs_ref, sel_ref, qw_ref, grad_ref, back_ref = buffers
    outs = {"mn": mn_ref, "md": md_ref, "di": di_ref, "ai": ai_ref, "as": as_ref}
    f = lambda a: float(np.float32(a))
    for c in late:
        c.wait()

    def halo(at, j, north=n_ref, south=s_ref):
        at = (*at, pl.ds(j, 4, stride=4), slice(None))
        return jnp.concatenate([north[at], south[at]], axis=0)

    rest = slice(32, E)
    mains, sides = [], []
    for z in range(5):
        for j in range(4):
            xe, xw, mod, rho = (halo((i, z), j, cn_ref, cs_ref) for i in (2, 3, 0, 1))
            vs = [halo((3 + c, z), j) for c in range(3)] + [expand(xe, xw, 3, 1)]
            ds = [halo((c, z), j) for c in range(3)] + [expand(xe, xw, 0, 1)]
            for ch in range(4):
                v_ref[ch][z, j, rest] = vs[ch]
                d_ref[ch][z, j, rest] = ds[ch] + DT * vs[ch]
            mods = [mod, expand(xe, xw, 6, 0)]
            rhos = [rho, strip_density(expand(xe, xw, 7, 0))]
            for m in range(2):

                def put(name, x):
                    at = (m, j, rest) if name in ("ai", "as") else (m, z, j, rest)
                    outs[name][at] = x

                fields(mods[m], rhos[m], j, z, put)
            mains.append(mods[0])
            sides.append(mods[1])
    c = east_coefs(jnp.concatenate(mains), jnp.concatenate(sides), sel_ref[...], qw_ref[...])
    for z in range(5):
        for j in range(4):
            at = (z * 4 + j) * 8
            ce_ref[z, j, rest] = c[at : at + 8] * (f(W[z]) * f(PERIODIC[j]))
    for m in range(2):
        for z in range(5):
            mn_ref[m, z, 4] = pltpu.roll(mn_ref[m, z, 0], E - 1, 0)

    row_forces(d_ref, halo_k, rest, slice(0, 8), 8, md_ref, ce_ref, grad_ref, back_ref)
    for ch in range(4):
        m = ch // 3
        for z in range(5):
            d = [d_ref[ch][z, j] for j in range(4)]
            g = slopes(d + [pltpu.roll(d[0], E - 1, 0)])
            r = tested([g[i] * mn_ref[m, z, i] for i in range(5)])
            r[0] = r[0] + pltpu.roll(r[4], 1, 0)
            for j in range(4):
                v = v_ref[ch][z, j]
                k = jnp.concatenate([own_k[ch][z, j], halo_k[ch][z, j]], axis=0) + r[j]
                if z == 0:
                    k = k + ai_ref[m, j] * v + as_ref[m, j] * d[j]
                v_ref[ch][z, j] = v - di_ref[m, z, j] * k


def prepare(fetched, halos, tables):
    grad, back, sel, qw = tables
    whole = pl.BlockSpec(memory_space=pltpu.VMEM)
    late = (*halos, sel, qw, grad, back)
    return pl.pallas_call(
        prepare_kernel,
        in_specs=[whole] * 18 + [pl.BlockSpec(memory_space=pltpu.HBM)] * 8,
        out_specs=[whole] * 14,
        out_shape=PREPARED,
        input_output_aliases={i: i for i in range(14)},
        scratch_shapes=[pltpu.VMEM((5, 4, 8, N), F32)] * 4
        + [pltpu.VMEM(x.shape, x.dtype) for x in late]
        + [pltpu.SemaphoreType.DMA((8,))],
        compiler_params=pltpu.CompilerParams(vmem_limit_bytes=VMEM_LIMIT),
        name="prepare",
    )(*fetched, *in_hbm(*late))


def steps_kernel(
    i0, i1, i2, i3, u0, u1, u2, u3, mn_ref, md_ref, di_ref, ce_ref, ai_ref, as_ref,
    b_ref, bs_ref, bn_ref, bo_ref, grad_ref, back_ref,
    dout_ref, vout_ref,
    d0, d1, d2, d3, v0, v1, v2, v3, k0, k1, k2, k3, n0, n1, n2, n3, f_ref,
):
    d_in, v_in = (i0, i1, i2, i3), (u0, u1, u2, u3)
    d_ref, v_ref = (d0, d1, d2, d3), (v0, v1, v2, v3)
    k_ref, kn_ref = (k0, k1, k2, k3), (n0, n1, n2, n3)
    for t in range(3):
        n, at = FORCE_ROWS[t]
        gap = jnp.zeros((8 - n // 2, N), F32)
        for ch in range(4):
            for j in range(4):
                own = pl.ds(j, 32, stride=4)
                x = b_ref[t, ch, own, :] if ch < 3 else bs_ref[t, own, :]
                halo = pl.ds(at + j, n // 4, stride=4)
                f_ref[t, ch, j] = jnp.concatenate(
                    [x, bn_ref[ch, halo, :], gap, bo_ref[ch, halo, :]], axis=0
                )
    for ch in range(3):
        for j in range(4):
            x = b_ref[3, ch, pl.ds(j, 32, stride=4), :]
            f_ref[3, ch, j] = jnp.concatenate([x, jnp.zeros((8, N), F32)], axis=0)

    for ch in range(4):
        for j in range(4):
            for z in range(5):
                v = v_in[ch][z, j]
                if z == 0:
                    v = v + di_ref[ch // 3, z, j] * f_ref[0, ch, j]
                v_ref[ch][z, j] = v
                d_ref[ch][z, j] = d_in[ch][z, j] + DT * v

    def velocity(t, ch, j, z, d, k):
        m = ch // 3
        n = slice(0, d.shape[0])
        v = v_ref[ch][z, j, n]
        if z == 0:
            k = k + ai_ref[m, j, n] * v + as_ref[m, j, n] * d - f_ref[t, ch, j, n]
        return v - di_ref[m, z, j, n] * k

    def step(t, carry):
        def emit(ch, j, z, d, k):
            v = velocity(t, ch, j, z, d, k)
            v_ref[ch][z, j] = v
            d_ref[ch][z, j] = d + DT * v

        line_forces(d_ref, k_ref, kn_ref, mn_ref, md_ref, ce_ref, grad_ref, back_ref, 4, emit)
        return carry

    lax.fori_loop(1, 3, step, 0)

    def final(ch, j, z, d, k):
        dout_ref[ch, z, pl.ds(j, 32, stride=4), :] = d
        vout_ref[ch, z, pl.ds(j, 32, stride=4), :] = velocity(3, ch, j, z, d, k)

    line_forces(d_ref, k_ref, kn_ref, mn_ref, md_ref, ce_ref, grad_ref, back_ref, 3, final)


def steps(prepared, b, bs, bn, bo, tables):
    grad, back = tables[:2]
    whole = pl.BlockSpec(memory_space=pltpu.VMEM)
    return pl.pallas_call(
        steps_kernel,
        in_specs=[whole] * 20,
        out_specs=[whole] * 2,
        out_shape=[jax.ShapeDtypeStruct((3, 5, N, N), F32)] * 2,
        scratch_shapes=[pltpu.VMEM((5, 4, E, N), F32)] * 16 + [pltpu.VMEM((4, 4, 4, E, N), F32)],
        compiler_params=pltpu.CompilerParams(vmem_limit_bytes=VMEM_LIMIT),
        name="steps",
    )(*prepared, b, bs, bn, bo, grad, back)


def local(displacement, velocity, modulus, density, traces, record_row):
    tables = tuple(jnp.asarray(t) for t in east_tables())
    west, east, north, south, late_north, late_south, sent = begin(
        displacement, velocity, modulus, density, jnp.transpose(traces[0], (1, 0, 2)), record_row
    )
    from_east = shifted(west, "reg", -1)
    from_west = shifted(east, "reg", 1)
    from_north = shifted(south, "src", -1)
    from_south = shifted(north, "src", 1)
    arrived = lax.all_to_all(
        sent.reshape(N, 40, N), ("src", "reg"), split_axis=0, concat_axis=0, tiled=True
    )
    corner = jnp.stack([from_east, from_west])
    late_south = jnp.concatenate([late_south, corner[:, :, :H]], axis=0)
    late_north = jnp.concatenate([late_north, corner[:, :, N - H :]], axis=0)
    corner_north = shifted(late_south, "src", -1)
    corner_south = shifted(late_north, "src", 1)
    co = coefs(modulus, density, from_east, from_west)
    own = early(displacement, velocity, modulus, density, from_east, from_west, tables)
    b, b_strip, b_north, b_south, *fetched = place(arrived, co, own)
    b_from_south = shifted(b_north, "src", 1)
    b_from_north = shifted(b_south, "src", -1)
    from_north, from_south, corner_north, corner_south, _ = lax.optimization_barrier(
        (from_north, from_south, corner_north, corner_south, b)
    )
    prepared = prepare(fetched, (from_north, from_south, corner_north, corner_south), tables)
    return steps(prepared, b, b_strip, b_from_north, b_from_south, tables)


def solution(mesh):
    state = P(None, None, "src", "reg")
    field = P(None, "src", "reg")
    in_specs = (state, state, field, field, P(("src", "reg"), None, None, None), P(("src", "reg"), None))
    return jax.shard_map(local, mesh=mesh, in_specs=in_specs, out_specs=(state, state), check_vma=False)
```

```python
import math

import jax
import jax.numpy as jnp
import numpy as np
from jax import lax
from jax.experimental import pallas as pl
from jax.experimental.pallas import tpu as pltpu
from jax.sharding import PartitionSpec as P


F32 = jnp.float32
BF16 = jnp.bfloat16
STEPS = 4
DT = 0.02
N = 128
H = 16
E = 40
FORCE_ROWS = ((12, 0), (8, 12), (4, 20))
VMEM_LIMIT = 28 * 1024 * 1024


def gll():
    inner = math.sqrt(3.0 / 7.0)
    x = np.array([-1.0, -inner, 0.0, inner, 1.0])
    w = np.array([0.1, 49.0 / 90.0, 32.0 / 45.0, 49.0 / 90.0, 0.1])
    leg = (35.0 * x**4 - 30.0 * x**2 + 3.0) / 8.0
    d = np.zeros((5, 5))
    for i in range(5):
        for j in range(5):
            if i != j:
                d[i, j] = leg[i] / (leg[j] * (x[i] - x[j]))
    d[0, 0] = -5.0
    d[4, 4] = 5.0
    return d, w


DER, W = gll()
PERIODIC = [2 * W[0], W[1], W[2], W[3]]


def network():
    odd = [[(DER[i, 0] - DER[i, 4]) / 2, (DER[i, 1] - DER[i, 3]) / 2] for i in (0, 1)]
    even = [[(DER[i, 0] + DER[i, 4]) / 2, (DER[i, 1] + DER[i, 3]) / 2] for i in (0, 1)]
    scale = [even[0][0], even[1][0], DER[2, 0]]
    f = lambda x: float(np.float32(x))
    p = [[f(odd[i][k] / scale[i]) for k in range(2)] for i in range(2)]
    q = [f(even[i][1] / scale[i]) for i in range(2)]
    scale = np.array(scale + scale[1::-1])
    return p, q, f(DER[2, 1] / DER[2, 0]), W * scale**2


ODD, EVEN, MIDDLE, POINT = network()


def slopes(v):
    twice = v[2] + v[2]
    u0, u1 = (v[0] + v[4]) - twice, (v[1] + v[3]) - twice
    m0, m1 = v[0] - v[4], v[1] - v[3]
    out = [None] * 5
    for i in (0, 1):
        p = ODD[i][0] * m0 + ODD[i][1] * m1
        q = u0 + EVEN[i] * u1
        out[i], out[4 - i] = p + q, p - q
    out[2] = m0 + MIDDLE * m1
    return out


def tested(f):
    ep, eq = [f[0] + f[4], f[1] + f[3]], [f[0] - f[4], f[1] - f[3]]
    m0 = (ODD[0][0] * ep[0] + ODD[1][0] * ep[1]) + f[2]
    m1 = (ODD[0][1] * ep[0] + ODD[1][1] * ep[1]) + MIDDLE * f[2]
    u0 = eq[0] + eq[1]
    u1 = EVEN[0] * eq[0] + EVEN[1] * eq[1]
    return [u0 + m0, u1 + m1, -2.0 * (u0 + u1), u1 - m1, u0 - m0]


def column_of(x, comp):
    if 0 <= x < N:
        return x
    return N + 32 * comp + (x - N if x >= N else x + 32)


def east_tables():
    grad = np.zeros((3, 256, 256))
    sel = np.zeros((256, 256))
    weight = np.zeros((1, 256))
    for k in range(E):
        for i in range(5):
            q = i * E + k
            xi = 4 * (k - 4) + i
            weight[0, q] = 0.5 * W[i]
            if xi < N + H:
                sel[column_of(xi, 0), q] = 1.0
            for comp in range(3):
                for j in range(5):
                    xj = 4 * (k - 4) + j
                    if xj < N + H:
                        grad[comp, column_of(xj, comp), q] = DER[i, j]

    def two(a):
        hi = a.astype(np.float32).astype(jnp.bfloat16)
        lo = (a - hi.astype(np.float64)).astype(np.float32).astype(jnp.bfloat16)
        return np.stack([hi, lo], axis=1)

    back = np.ascontiguousarray(np.swapaxes(grad, 1, 2))
    return two(grad), two(back), sel.astype(jnp.bfloat16), weight.astype(np.float32)


def shifted(block, axis, distance):
    n = lax.axis_size(axis)
    return lax.ppermute(block, axis, [((i - distance) % n, i) for i in range(n)])


def in_hbm(*arrays):
    return [pltpu.with_memory_space_constraint(x, pltpu.HBM) for x in arrays]


def dot(a, b):
    return jnp.dot(a, b, preferred_element_type=F32)


def split2(x):
    hi = x.astype(BF16)
    return hi, (x - hi.astype(F32)).astype(BF16)


def lane_ids(shape):
    return lax.broadcasted_iota(jnp.int32, shape, len(shape) - 1)


def east_weight(shape):
    r = lane_ids(shape) % 4
    f = lambda a: float(np.float32(a))
    return jnp.where(r == 0, f(PERIODIC[0]), jnp.where(r == 2, f(PERIODIC[2]), f(PERIODIC[1])))


def moved(x, shift):
    return pltpu.roll(x, shift % N, x.ndim - 1) if shift % N else x


def lane_move(x, shift, start, width=16):
    shift %= 128
    y = pltpu.roll(x, shift, x.ndim - 1) if shift else x
    lane = lane_ids(x.shape)
    return jnp.where((lane >= start) & (lane < start + width), y, 0.0)


WEST_GROUPS = ((0, 12, 116, 0), (21, 8, 120, 1), (34, 4, 124, 2))
EAST_GROUPS = ((12, 9, 0, 0), (29, 5, 0, 1), (38, 1, 0, 2))
TO_WEST = (0, 32, 64, 96, 16, 48, 80, 112)
TO_EAST = (112, 16, 48, 80, 0, 32, 64, 96)


def begin_kernel(
    d_ref, v_ref, m_ref, r_ref, tr_ref, id_ref,
    west_ref, east_ref, north_ref, south_ref, ln_ref, ls_ref, sent_ref,
    buf, west_buf, east_buf, tr_buf, sent_buf, id_buf, row_buf, in_sem, row_sem, out_sem, tr_sem, sent_sem,
):
    copy = pltpu.make_async_copy
    face_rows = copy(id_ref, row_buf, sent_sem.at[8])
    face_rows.start()
    loads = []
    for z in range(5):
        loads.append(
            [
                copy(d_ref.at[:, z], buf.at[z, 0:3], in_sem.at[z, 0]),
                copy(v_ref.at[:, z], buf.at[z, 3:6], in_sem.at[z, 1]),
                copy(m_ref.at[z], buf.at[z, 6], in_sem.at[z, 2]),
                copy(r_ref.at[z], buf.at[z, 7], in_sem.at[z, 3]),
            ]
        )
        for c in loads[z]:
            c.start()
    records = []
    for g in range(8):
        at = pl.ds(64 * g, 64)
        records.append(copy(tr_ref.at[:, at], tr_buf.at[:, at], tr_sem.at[g]))
        records[g].start()
    lane = lane_ids((N, N))
    stores = []
    for z in range(5):
        for c in loads[z]:
            c.wait()
        for i, (at, top, low) in enumerate(
            ((slice(0, 6), north_ref, south_ref), (slice(6, 8), ln_ref, ls_ref))
        ):
            stores.append(copy(buf.at[z, at, N - H : N], top.at[:, z], row_sem.at[z, 2 * i]))
            stores.append(copy(buf.at[z, at, 0:H], low.at[:, z], row_sem.at[z, 2 * i + 1]))
        for c in stores[-4:]:
            c.start()
        packed = []
        for h in range(2):
            x = buf[z, 4 * h]
            for a in range(1, 4):
                mask = (lane >= 32 * a - 16) & (lane < 32 * a + 16)
                x = jnp.where(mask, pltpu.roll(buf[z, 4 * h + a], 32 * a, 1), x)
            packed.append(x)
        other = pltpu.roll(packed[1], 16, 1)
        west_buf[z] = jnp.where(lane % 32 < 16, packed[0], other)
        east_buf[z] = jnp.where(lane % 32 < 16, other, packed[0])
        stores.append(copy(west_buf.at[z], west_ref.at[z], out_sem.at[z, 0]))
        stores.append(copy(east_buf.at[z], east_ref.at[z], out_sem.at[z, 1]))
        for c in stores[-2:]:
            c.start()
    face_rows.wait()
    mine = lane_ids((N, 4 * N)) // STEPS == lax.broadcasted_iota(jnp.int32, (N, 4 * N), 0)
    spread = jnp.where(mine, jnp.broadcast_to(row_buf[...].astype(F32), (N, 4 * N)), 0.0).astype(BF16)
    step = lax.broadcasted_iota(jnp.int32, (4 * N, N), 0) % STEPS == lane_ids((4 * N, N))
    id_buf[...] = dot(spread, jnp.where(step, 1.0, 0.0).astype(BF16))
    lane = lane_ids((16, N))
    for g in range(8):
        records[g].wait()
        first = 640 * g
        for d in range(16):
            for k in range(9):
                sent_buf[pl.ds(first + 40 * d + 4 * k, 4), :] = tr_buf[k, pl.ds(64 * g + 4 * d, 4), :]
        ids = id_buf[16 * g : 16 * g + 16, :]
        ids = (
            ids
            + pltpu.roll(pltpu.roll(ids, 1, 0), 4, 1)
            + pltpu.roll(pltpu.roll(ids, 15, 0), 8, 1)
        )
        extra = [ids]
        for rho in range(3):
            sides = [jnp.zeros((16, N), F32)] * 2
            for c in range(3):
                for t in range(3):
                    x = tr_buf[3 * rho + c, pl.ds(64 * g + t, 16, stride=4), :]
                    for i, groups in enumerate((WEST_GROUPS, EAST_GROUPS)):
                        off, width, col, _ = groups[t]
                        at = 40 * c + off
                        y = pltpu.roll(x, (at - col) % N, 1) if (at - col) % N else x
                        sides[i] = jnp.where((lane >= at) & (lane < at + width), y, sides[i])
            extra.append(pltpu.roll(sides[0], 1, 0) + pltpu.roll(sides[1], 15, 0))
        for i, x in enumerate(extra):
            for h in range(2):
                sent_buf[pl.ds(first + 320 * h + 36 + i, 8, stride=40), :] = x[8 * h : 8 * h + 8]
        at = pl.ds(first, 640)
        stores.append(copy(sent_buf.at[at], sent_ref.at[at], sent_sem.at[g]))
        stores[-1].start()
    for c in stores:
        c.wait()


def begin(d, v, m, r, records, ids):
    hbm = pl.BlockSpec(memory_space=pltpu.HBM)
    dma = pltpu.SemaphoreType.DMA
    return pl.pallas_call(
        begin_kernel,
        in_specs=[hbm] * 6,
        out_specs=[hbm] * 7,
        out_shape=[pltpu.HBM((5, N, N), F32)] * 2
        + [pltpu.HBM((6, 5, H, N), F32)] * 2
        + [pltpu.HBM((2, 5, H, N), F32)] * 2
        + [pltpu.HBM((40 * N, N), F32)],
        scratch_shapes=[
            pltpu.VMEM((5, 8, N, N), F32),
            pltpu.VMEM((5, N, N), F32),
            pltpu.VMEM((5, N, N), F32),
            pltpu.VMEM((9, 4 * N, N), F32),
            pltpu.VMEM((40 * N, N), F32),
            pltpu.VMEM((N, N), F32),
            pltpu.VMEM((1, STEPS * N), jnp.int32),
            dma((5, 4)),
            dma((5, 4)),
            dma((5, 2)),
            dma((8,)),
            dma((9,)),
        ],
        compiler_params=pltpu.CompilerParams(vmem_limit_bytes=20 * 1024 * 1024),
        name="begin",
    )(*in_hbm(d, v, m, r, records, ids))


def coefs_kernel(m_ref, r_ref, re_ref, rw_ref, out_ref):
    f = lambda a: float(np.float32(a))
    shape = (N, N)
    lane = lane_ids(shape)
    row = lax.broadcasted_iota(jnp.int32, shape, 0) % 4
    pick = lambda n: jnp.where(
        n == 0, f(PERIODIC[0]), jnp.where(n == 2, f(PERIODIC[2]), f(PERIODIC[1]))
    )

    def three(at, mod, rho, ew):
        area = 0.25 * ew * pick(row)
        out_ref[at] = area
        out_ref[at + 1] = area * jnp.sqrt(rho * mod)
        out_ref[at + 2] = area * (0.5 * mod)

    three(0, m_ref[0], r_ref[0], pick(lane % 4))
    mod = rho = jnp.ones(shape, F32)
    node = jnp.zeros(shape, jnp.int32)
    for groups, src, base, at_lane in (
        (WEST_GROUPS, rw_ref[0], 112, TO_EAST),
        (EAST_GROUPS, re_ref[0], 0, TO_WEST),
    ):
        for c in range(3):
            for off, width, col, _ in groups:
                at = 40 * c + off
                mask = (lane >= at) & (lane < at + width)
                mod = jnp.where(mask, moved(src, at - at_lane[6] - (col - base)), mod)
                rho = jnp.where(mask, moved(src, at - at_lane[7] - (col - base)), rho)
                node = jnp.where(mask, lane - at, node)
    three(3, mod, rho, pick(node % 4))


def coefs(m, r, re, rw):
    plane = pl.BlockSpec((1, N, N), lambda i: (0, 0, 0))
    return pl.pallas_call(
        coefs_kernel,
        grid=(1,),
        in_specs=[plane] * 4,
        out_specs=pl.BlockSpec((6, N, N), lambda i: (0, 0, 0)),
        out_shape=jax.ShapeDtypeStruct((6, N, N), F32),
        name="coefs",
    )(m, r, re, rw)


def place_kernel(*refs):
    (arr_ref, co_hbm), own, refs = refs[:2], refs[2:11], refs[11:]
    (b_ref, strip_ref, north_ref, south_ref), fetched, refs = refs[:4], refs[4:22], refs[22:]
    inj_ref, side_ref, vid_ref, ids_ref, co_ref, sem, own_sem = refs
    copy = pltpu.make_async_copy
    lane = lane_ids((N, N))
    plane = jnp.where(lane < 8, lane % 4, lane - 5)
    slot = jnp.where(lane < 4, 16, 8)
    where_to = (arr_ref[:, 36, :].astype(jnp.int32) + N * plane) * slot
    vid_ref[...] = jnp.transpose(where_to)[:16]
    to_scalar = copy(vid_ref, ids_ref, sem.at[0])
    to_scalar.start()
    to_co = copy(co_hbm, co_ref, sem.at[1])
    to_co.start()
    node = pl.ds(0, 32)
    moves = []
    for ch in range(4):
        moves.append((own[0].at[ch], fetched[ch].at[:, :, node]))
        moves.append((own[1].at[ch], fetched[4 + ch].at[:, :, node]))
    for m in range(2):
        moves.append((own[2].at[m], fetched[8].at[m, :, 0:4, node]))
        moves.append((own[3].at[m], fetched[9].at[m, :, :, node]))
        moves.append((own[4].at[m], fetched[10].at[m, :, :, node]))
    for i in (5, 6, 7):
        moves.append((own[i], fetched[6 + i].at[:, :, node]))
    moves.extend((own[8].at[ch], fetched[14 + ch]) for ch in range(4))
    moves = [copy(x, y, own_sem.at[i]) for i, (x, y) in enumerate(moves)]
    to_scalar.wait()
    for c in moves:
        c.start()

    def body(s, carry):
        tail = arr_ref[s, 32:40, :]
        for t in range(STEPS):
            at = pl.multiple_of(ids_ref[t, s], 16)
            inj_ref[pl.ds(at, 8), :] = arr_ref[s, pl.ds(t, 8, stride=4), :]
            inj_ref[pl.ds(at + 8, 8), :] = tail
        for i in range(2):
            for t in range(3):
                side_ref[pl.ds(pl.multiple_of(ids_ref[4 + 4 * i + t, s], 8), 8), :] = tail
        return carry

    lax.fori_loop(0, 128, body, 0, unroll=8)
    to_co.wait()
    lane = lane_ids((8, N))

    def combine(k, carry):
        y = pl.multiple_of(k * 8, 8)
        rows = pl.ds(y, 8)
        co = [co_ref[i, rows, :] for i in range(6)]
        for t in range(STEPS):
            for c in range(3):
                base = (t * N + y) * 16
                inc = inj_ref[pl.ds(base + c, 8, stride=16), :]
                vel = inj_ref[pl.ds(base + 3 + c, 8, stride=16), :]
                dis = inj_ref[pl.ds(base + (6 + c if c < 2 else 8 + t), 8, stride=16), :]
                b_ref[t, c, rows, :] = co[0] * inc + co[1] * vel + co[2] * dis
        b = None
        for rho in range(3):
            x = jnp.zeros((8, N), F32)
            for i, groups in enumerate((WEST_GROUPS, EAST_GROUPS)):
                for off, width, _, t in groups:
                    part = side_ref[pl.ds(((3 * i + t) * N + y) * 8 + 5 + rho, 8, stride=8), :]
                    mask = (lane >= off) & (lane < off + width)
                    for c in (1, 2):
                        mask = mask | ((lane >= 40 * c + off) & (lane < 40 * c + off + width))
                    x = jnp.where(mask, part, x)
            b = co[3] * x if b is None else b + co[3 + rho] * x
        for t in range(3):
            out = None
            for c in range(3):
                off, width, col, _ = WEST_GROUPS[t]
                start = 32 * c + 16 + col - 112
                p = lane_move(b, start - 40 * c - off, start, width)
                off, width, _, _ = EAST_GROUPS[t]
                p = p + lane_move(b, 32 * c - 40 * c - off, 32 * c, width)
                out = p if out is None else out + p
            strip_ref[t, rows, :] = out
        return carry

    lax.fori_loop(0, 16, combine, 0)
    for t in range(3):
        n, at = FORCE_ROWS[t]
        for ch in range(4):
            x = b_ref.at[t, ch] if ch < 3 else strip_ref.at[t]
            north_ref[ch, at : at + n] = x[N - n :, :]
            south_ref[ch, at : at + n] = x[:n, :]
    for c in moves:
        c.wait()


PREPARED = (
    *[jax.ShapeDtypeStruct((5, 4, E, N), F32)] * 8,
    jax.ShapeDtypeStruct((2, 5, 5, E, N), F32),
    jax.ShapeDtypeStruct((2, 5, 4, E, N), F32),
    jax.ShapeDtypeStruct((2, 5, 4, E, N), F32),
    jax.ShapeDtypeStruct((5, 4, E, 256), F32),
    jax.ShapeDtypeStruct((2, 4, E, N), F32),
    jax.ShapeDtypeStruct((2, 4, E, N), F32),
)


def place(arrived, co, own):
    whole = pl.BlockSpec(memory_space=pltpu.VMEM)
    return pl.pallas_call(
        place_kernel,
        in_specs=[whole] + [pl.BlockSpec(memory_space=pltpu.HBM)] * 10,
        out_specs=[whole] * 22,
        out_shape=[
            jax.ShapeDtypeStruct((STEPS, 3, N, N), F32),
            jax.ShapeDtypeStruct((3, N, N), F32),
            jax.ShapeDtypeStruct((4, 24, N), F32),
            jax.ShapeDtypeStruct((4, 24, N), F32),
            *PREPARED,
            *[jax.ShapeDtypeStruct((5, 4, 32, N), F32)] * 4,
        ],
        scratch_shapes=[
            pltpu.VMEM((STEPS * N * 16, N), F32),
            pltpu.VMEM((6 * N * 8, N), F32),
            pltpu.VMEM((16, N), jnp.int32),
            pltpu.SMEM((16, N), jnp.int32),
            pltpu.VMEM((6, N, N), F32),
            pltpu.SemaphoreType.DMA((2,)),
            pltpu.SemaphoreType.DMA((21,)),
        ],
        compiler_params=pltpu.CompilerParams(vmem_limit_bytes=VMEM_LIMIT),
        name="place",
    )(arrived, *in_hbm(co, *own))


def line_forces(d, k, kn, mn_ref, md_ref, ce_ref, grad_ref, back_ref, channels, emit):
    live = E if channels == 4 else 32
    rows = 5 * 4 * live

    def north(ch):
        m = ch // 3
        for z in range(5):
            v = [d[ch][z, j] for j in range(4)]
            v.append(pltpu.roll(v[0], E - 1, 0))
            g = slopes(v)
            r = tested([g[i] * mn_ref[m, z, i] for i in range(5)])
            r[0] = r[0] + pltpu.roll(r[4], 1, 0)
            for j in range(4):
                kn[ch][z, j] = r[j]

    def depth(ch):
        m = ch // 3
        for j in range(4):
            x = [d[ch][z, j, :live] for z in range(5)]
            g = slopes(x)
            r = tested([g[z] * md_ref[m, z, j, :live] for z in range(5)])
            for z in range(5):
                emit(ch, j, z, x[z], (k[ch][z, j, :live] + kn[ch][z, j, :live]) + r[z])

    sh, sl = split2(d[3][:, :, :live].reshape(rows, N))
    strip = None
    for c in range(3):
        mh, ml = split2(d[c][:, :, :live].reshape(rows, N))
        hi = jnp.concatenate([mh, sh], axis=1)
        lo = jnp.concatenate([ml, sl], axis=1)
        g = dot(hi, grad_ref[c, 0]) + dot(lo, grad_ref[c, 0]) + dot(hi, grad_ref[c, 1])
        fh, fl = split2(g * ce_ref[:, :, :live].reshape(rows, 256))
        f = dot(fh, back_ref[c, 0]) + dot(fl, back_ref[c, 0]) + dot(fh, back_ref[c, 1])
        k[c][:, :, :live] = f[:, :N].reshape(5, 4, live, N)
        if channels == 4:
            strip = f[:, N:] if strip is None else strip + f[:, N:]
        north(c)
        if c:
            depth(c - 1)
    if channels == 4:
        north(3)
        k[3][...] = strip.reshape(5, 4, E, N)
    depth(2)
    if channels == 4:
        depth(3)


def row_forces(d, k, at, into, n, md_ref, ce_ref, grad_ref, back_ref):
    rows = 5 * 4 * n
    sh, sl = split2(d[3][:, :, at].reshape(rows, N))
    strip = None
    for c in range(3):
        mh, ml = split2(d[c][:, :, at].reshape(rows, N))
        hi = jnp.concatenate([mh, sh], axis=1)
        lo = jnp.concatenate([ml, sl], axis=1)
        g = dot(hi, grad_ref[c, 0]) + dot(lo, grad_ref[c, 0]) + dot(hi, grad_ref[c, 1])
        fh, fl = split2(g * ce_ref[:, :, at].reshape(rows, 256))
        f = dot(fh, back_ref[c, 0]) + dot(fl, back_ref[c, 0]) + dot(fh, back_ref[c, 1])
        k[c][:, :, into] = f[:, :N].reshape(5, 4, n, N)
        strip = f[:, N:] if strip is None else strip + f[:, N:]
    k[3][:, :, into] = strip.reshape(5, 4, n, N)
    for ch in range(4):
        for j in range(4):
            g = slopes([d[ch][z, j, at] for z in range(5)])
            r = tested([g[z] * md_ref[ch // 3, z, j, at] for z in range(5)])
            for z in range(5):
                k[ch][z, j, into] = k[ch][z, j, into] + r[z]


def north_update(ch, d_ref, mn_ref, own_k, halo_k, emit):
    for z in range(5):
        d = [d_ref[ch][z, j] for j in range(4)]
        g = slopes(d + [pltpu.roll(d[0], E - 1, 0)])
        r = tested([g[i] * mn_ref[ch // 3, z, i] for i in range(5)])
        r[0] = r[0] + pltpu.roll(r[4], 1, 0)
        for j in range(4):
            k = jnp.concatenate([own_k[ch][z, j], halo_k[ch][z, j]], axis=0) + r[j]
            emit(ch, j, z, d[j], k)


def expand(xe, xw, first, step):
    out = None
    for c in range(3):
        p = lane_move(xe, 32 * c - TO_WEST[first + step * c], 32 * c)
        p = p + lane_move(xw, 32 * c + 16 - TO_EAST[first + step * c], 32 * c + 16)
        out = p if out is None else out + p
    return out


def fields(mod, rho, j, z, put):
    f = lambda a: float(np.float32(a))
    ew = east_weight(mod.shape)
    half = 0.5 * mod * ew
    put("mn", half * f(POINT[j] * W[z]))
    put("md", half * f(POINT[z] * PERIODIC[j]))
    put("di", DT / (0.125 * rho * ew * (f(PERIODIC[j]) * f(W[z]))))
    if z == 0:
        area = 0.25 * ew * f(PERIODIC[j])
        put("ai", area * jnp.sqrt(rho * mod))
        put("as", area * (0.5 * mod))


def east_coefs(main, strip, sel, weight):
    x = jnp.concatenate([main, strip], axis=1)
    hi = x.astype(BF16)
    mid, lo = split2(x - hi.astype(F32))
    return (dot(hi, sel) + dot(mid, sel) + dot(lo, sel)) * weight


def strip_density(rho):
    return jnp.where(lane_ids(rho.shape) < 96, rho, 1.0)


def early_kernel(
    d_ref, v_ref, m_ref, r_ref, re_ref, rw_ref, sel_ref, qw_ref, grad_ref, back_ref,
    d_out, v_out, mn_out, md_out, di_out, ce_out, ai_out, as_out, k_out,
):
    f = lambda a: float(np.float32(a))
    outs = {"mn": mn_out, "md": md_out, "di": di_out, "ai": ai_out, "as": as_out}

    def plane(z):
        for j in range(4):
            own = pl.ds(j, 32, stride=4)
            xe, xw = re_ref[z, own, :], rw_ref[z, own, :]
            vs = [v_ref[c, z, own, :] for c in range(3)] + [expand(xe, xw, 3, 1)]
            ds = [d_ref[c, z, own, :] for c in range(3)] + [expand(xe, xw, 0, 1)]
            for ch in range(4):
                v_out[ch, z, j] = vs[ch]
                d_out[ch, z, j] = ds[ch] + DT * vs[ch]
            mods = [m_ref[z, own, :], expand(xe, xw, 6, 0)]
            rhos = [r_ref[z, own, :], strip_density(expand(xe, xw, 7, 0))]
            for m in range(2):

                def put(name, x):
                    at = (m, j) if name in ("ai", "as") else (m, z, j)
                    outs[name][at] = x

                fields(mods[m], rhos[m], j, z, put)
            weight = qw_ref[...] * (f(W[z]) * f(PERIODIC[j]))
            ce_out[z, j] = east_coefs(mods[0], mods[1], sel_ref[...], weight)

    for z in range(5):
        plane(z)
    node = slice(0, 32)
    d, k = [d_out.at[ch] for ch in range(4)], [k_out.at[ch] for ch in range(4)]
    row_forces(d, k, node, node, 32, md_out, ce_out, grad_ref, back_ref)


OWN_SHAPES = (
    *((4, 5, 4, 32, N),) * 2,
    *((2, 5, 4, 32, N),) * 3,
    (5, 4, 32, 256),
    *((2, 4, 32, N),) * 2,
    (4, 5, 4, 32, N),
)


def early(d, v, m, r, re, rw, tables):
    grad, back, sel, qw = tables
    whole = pl.BlockSpec(memory_space=pltpu.VMEM)
    return pl.pallas_call(
        early_kernel,
        in_specs=[whole] * 10,
        out_specs=[whole] * 9,
        out_shape=[jax.ShapeDtypeStruct(x, F32) for x in OWN_SHAPES],
        compiler_params=pltpu.CompilerParams(vmem_limit_bytes=16 * 1024 * 1024),
        name="early",
    )(d, v, m, r, re, rw, sel, qw, grad, back)


def prepare_kernel(*refs):
    own_k, (b_ref, strip_ref), halos, tables, refs = (
        refs[14:18], refs[18:20], refs[20:24], refs[24:28], refs[28:]
    )
    (d0, d1, d2, d3, v0, v1, v2, v3), refs = refs[:8], refs[8:]
    (mn_ref, md_ref, di_ref, ce_ref, ai_ref, as_ref), next_k, refs = refs[:6], refs[6:10], refs[10:]
    halo_k, refs = refs[:4], refs[4:]
    buffers, (halo_sem,) = refs[:8], refs[8:]
    d_ref, v_ref = (d0, d1, d2, d3), (v0, v1, v2, v3)
    copy = pltpu.make_async_copy
    late = [copy(x, y, halo_sem.at[i]) for i, (x, y) in enumerate(zip((*halos, *tables), buffers))]
    for c in late:
        c.start()
    n_ref, s_ref, cn_ref, cs_ref, sel_ref, qw_ref, grad_ref, back_ref = buffers
    outs = {"mn": mn_ref, "md": md_ref, "di": di_ref, "ai": ai_ref, "as": as_ref}
    f = lambda a: float(np.float32(a))
    for c in late:
        c.wait()

    def halo(at, j, north=n_ref, south=s_ref):
        at = (*at, pl.ds(j, 4, stride=4), slice(None))
        return jnp.concatenate([north[at], south[at]], axis=0)

    rest = slice(32, E)
    mains, sides = [], []
    for z in range(5):
        for j in range(4):
            xe, xw, mod, rho = (halo((i, z), j, cn_ref, cs_ref) for i in (2, 3, 0, 1))
            vs = [halo((3 + c, z), j) for c in range(3)] + [expand(xe, xw, 3, 1)]
            ds = [halo((c, z), j) for c in range(3)] + [expand(xe, xw, 0, 1)]
            for ch in range(4):
                v_ref[ch][z, j, rest] = vs[ch]
                d_ref[ch][z, j, rest] = ds[ch] + DT * vs[ch]
            mods = [mod, expand(xe, xw, 6, 0)]
            rhos = [rho, strip_density(expand(xe, xw, 7, 0))]
            for m in range(2):

                def put(name, x):
                    at = (m, j, rest) if name in ("ai", "as") else (m, z, j, rest)
                    outs[name][at] = x

                fields(mods[m], rhos[m], j, z, put)
            mains.append(mods[0])
            sides.append(mods[1])
    c = east_coefs(jnp.concatenate(mains), jnp.concatenate(sides), sel_ref[...], qw_ref[...])
    for z in range(5):
        for j in range(4):
            at = (z * 4 + j) * 8
            ce_ref[z, j, rest] = c[at : at + 8] * (f(W[z]) * f(PERIODIC[j]))
    for m in range(2):
        for z in range(5):
            mn_ref[m, z, 4] = pltpu.roll(mn_ref[m, z, 0], E - 1, 0)

    row_forces(d_ref, halo_k, rest, slice(0, 8), 8, md_ref, ce_ref, grad_ref, back_ref)

    def emit(ch, j, z, d, k):
        m = ch // 3
        v = v_ref[ch][z, j]
        if z == 0:
            k = k + ai_ref[m, j] * v + as_ref[m, j] * d
        v_ref[ch][z, j] = v - di_ref[m, z, j] * k

    for ch in range(4):
        north_update(ch, d_ref, mn_ref, own_k, halo_k, emit)
    node = slice(0, 32)
    for ch in range(4):
        for j in range(4):
            own = pl.ds(j, 32, stride=4)
            x = b_ref[0, ch, own, :] if ch < 3 else strip_ref[0, own, :]
            for z in range(5):
                v = v_ref[ch][z, j, node]
                if z == 0:
                    v = v + di_ref[ch // 3, z, j, node] * x
                    v_ref[ch][z, j, node] = v
                d_ref[ch][z, j, node] = d_ref[ch][z, j, node] + DT * v
    row_forces(d_ref, next_k, node, node, 32, md_ref, ce_ref, grad_ref, back_ref)


def prepare(fetched, b, strip, halos, tables):
    grad, back, sel, qw = tables
    whole = pl.BlockSpec(memory_space=pltpu.VMEM)
    late = (*halos, sel, qw, grad, back)
    return pl.pallas_call(
        prepare_kernel,
        in_specs=[whole] * 20 + [pl.BlockSpec(memory_space=pltpu.HBM)] * 8,
        out_specs=[whole] * 18,
        out_shape=(*PREPARED, *[jax.ShapeDtypeStruct((5, 4, 32, N), F32)] * 4),
        input_output_aliases={i: i for i in range(14)},
        scratch_shapes=[pltpu.VMEM((5, 4, 8, N), F32)] * 4
        + [pltpu.VMEM(x.shape, x.dtype) for x in late]
        + [pltpu.SemaphoreType.DMA((8,))],
        compiler_params=pltpu.CompilerParams(vmem_limit_bytes=VMEM_LIMIT),
        name="prepare",
    )(*fetched, b, strip, *in_hbm(*late))


def steps_kernel(
    i0, i1, i2, i3, u0, u1, u2, u3, mn_ref, md_ref, di_ref, ce_ref, ai_ref, as_ref,
    o0, o1, o2, o3, b_ref, bs_ref, bn_ref, bo_ref, grad_ref, back_ref,
    dout_ref, vout_ref,
    d0, d1, d2, d3, v0, v1, v2, v3, k0, k1, k2, k3, n0, n1, n2, n3, f_ref, *halo_k,
):
    d_in, v_in = (i0, i1, i2, i3), (u0, u1, u2, u3)
    d_ref, v_ref = (d0, d1, d2, d3), (v0, v1, v2, v3)
    k_ref, kn_ref = (k0, k1, k2, k3), (n0, n1, n2, n3)
    for t in range(3):
        n, at = FORCE_ROWS[t]
        gap = jnp.zeros((8 - n // 2, N), F32)
        for ch in range(4):
            for j in range(4):
                own = pl.ds(j, 32, stride=4)
                x = b_ref[t, ch, own, :] if ch < 3 else bs_ref[t, own, :]
                halo = pl.ds(at + j, n // 4, stride=4)
                f_ref[t, ch, j] = jnp.concatenate(
                    [x, bn_ref[ch, halo, :], gap, bo_ref[ch, halo, :]], axis=0
                )
    for ch in range(3):
        for j in range(4):
            x = b_ref[3, ch, pl.ds(j, 32, stride=4), :]
            f_ref[3, ch, j] = jnp.concatenate([x, jnp.zeros((8, N), F32)], axis=0)

    node, rest = slice(0, 32), slice(32, E)
    for ch in range(4):
        for j in range(4):
            for z in range(5):
                v_ref[ch][z, j, node] = v_in[ch][z, j, node]
                d_ref[ch][z, j, node] = d_in[ch][z, j, node]
                v = v_in[ch][z, j, rest]
                if z == 0:
                    v = v + di_ref[ch // 3, z, j, rest] * f_ref[0, ch, j, rest]
                v_ref[ch][z, j, rest] = v
                d_ref[ch][z, j, rest] = d_in[ch][z, j, rest] + DT * v

    def velocity(t, ch, j, z, d, k):
        m = ch // 3
        n = slice(0, d.shape[0])
        v = v_ref[ch][z, j, n]
        if z == 0:
            k = k + ai_ref[m, j, n] * v + as_ref[m, j, n] * d - f_ref[t, ch, j, n]
        return v - di_ref[m, z, j, n] * k

    def emit(t):
        def put(ch, j, z, d, k):
            v = velocity(t, ch, j, z, d, k)
            v_ref[ch][z, j] = v
            d_ref[ch][z, j] = d + DT * v

        return put

    row_forces(d_ref, halo_k, rest, slice(0, 8), 8, md_ref, ce_ref, grad_ref, back_ref)
    for ch in range(4):
        north_update(ch, d_ref, mn_ref, (o0, o1, o2, o3), halo_k, emit(1))
    line_forces(d_ref, k_ref, kn_ref, mn_ref, md_ref, ce_ref, grad_ref, back_ref, 4, emit(2))

    def final(ch, j, z, d, k):
        dout_ref[ch, z, pl.ds(j, 32, stride=4), :] = d
        vout_ref[ch, z, pl.ds(j, 32, stride=4), :] = velocity(3, ch, j, z, d, k)

    line_forces(d_ref, k_ref, kn_ref, mn_ref, md_ref, ce_ref, grad_ref, back_ref, 3, final)


def steps(prepared, b, bs, bn, bo, tables):
    grad, back = tables[:2]
    whole = pl.BlockSpec(memory_space=pltpu.VMEM)
    return pl.pallas_call(
        steps_kernel,
        in_specs=[whole] * 24,
        out_specs=[whole] * 2,
        out_shape=[jax.ShapeDtypeStruct((3, 5, N, N), F32)] * 2,
        scratch_shapes=[pltpu.VMEM((5, 4, E, N), F32)] * 16
        + [pltpu.VMEM((4, 4, 4, E, N), F32)]
        + [pltpu.VMEM((5, 4, 8, N), F32)] * 4,
        compiler_params=pltpu.CompilerParams(vmem_limit_bytes=VMEM_LIMIT),
        name="steps",
    )(*prepared, b, bs, bn, bo, grad, back)


def local(displacement, velocity, modulus, density, traces, record_row):
    tables = tuple(jnp.asarray(t) for t in east_tables())
    west, east, north, south, late_north, late_south, sent = begin(
        displacement, velocity, modulus, density, jnp.transpose(traces[0], (1, 0, 2)), record_row
    )
    from_east = shifted(west, "reg", -1)
    from_west = shifted(east, "reg", 1)
    from_north = shifted(south, "src", -1)
    from_south = shifted(north, "src", 1)
    arrived = lax.all_to_all(
        sent.reshape(N, 40, N), ("src", "reg"), split_axis=0, concat_axis=0, tiled=True
    )
    corner = jnp.stack([from_east, from_west])
    late_south = jnp.concatenate([late_south, corner[:, :, :H]], axis=0)
    late_north = jnp.concatenate([late_north, corner[:, :, N - H :]], axis=0)
    corner_north = shifted(late_south, "src", -1)
    corner_south = shifted(late_north, "src", 1)
    co = coefs(modulus, density, from_east, from_west)
    own = early(displacement, velocity, modulus, density, from_east, from_west, tables)
    b, b_strip, b_north, b_south, *fetched = place(arrived, co, own)
    b_from_south = shifted(b_north, "src", 1)
    b_from_north = shifted(b_south, "src", -1)
    from_north, from_south, corner_north, corner_south, _ = lax.optimization_barrier(
        (from_north, from_south, corner_north, corner_south, b)
    )
    prepared = prepare(fetched, b, b_strip, (from_north, from_south, corner_north, corner_south), tables)
    return steps(prepared, b, b_strip, b_from_north, b_from_south, tables)


def solution(mesh):
    state = P(None, None, "src", "reg")
    field = P(None, "src", "reg")
    in_specs = (state, state, field, field, P(("src", "reg"), None, None, None), P(("src", "reg"), None))
    return jax.shard_map(local, mesh=mesh, in_specs=in_specs, out_specs=(state, state), check_vma=False)
```
